32 devices in a mesh: win: 4 (over x, core), tile: 8 (over z, y).
Axes of the slice: x: 2, y: 2, z: 4, core: 2. Of those that a mesh axis runs over, the one named last changes fastest.
Arguments:
- increment: float32 [4, 128, 256, 512], P('win', None, 'tile'), may hold values from -6 to 6
- diffusivity: float32 [4, 256, 512], P('win', 'tile'), may hold values from 0.04 to 0.2
- wind: float32 [4, 128], P('win'), may hold values from -0.3 to 0.3
- vertical_cov: bfloat16 [128, 128], replicated, may hold values from -1 to 2, as said below
- row_cov: bfloat16 [256, 256], replicated, may hold values from -1 to 2, as said below
- column_cov: bfloat16 [512, 512], replicated, may hold values from -1 to 2, as said below
Outputs:
- covaried: float32 [4, 128, 256, 512], P('win', 'tile')
The draws below stay inside these ranges and needn't reach their ends.
Inputs may be any that keep to these rules, and one draw needn't show every extreme that they name: `vertical_cov`: symmetric and positive definite. `row_cov`: symmetric and positive definite. `column_cov`: symmetric and positive definite.
All inputs are finite; a program needn't handle non-finite values.
Results may differ from the reference program's by a relative error of at most 0.0003.
Values sent between devices are 32-bit elements; how exact they have to be, the bound alone decides.
No kernel may reach another device: no remote copies, remote signals or barrier semaphores. Data moves between devices by JAX's collectives and lax.ppermute only.
A program may use at most 128 MiB of HBM per device.

```python
import jax
import jax.numpy as jnp
from jax import lax

L = 128
NY = 256
NX = 512
STEPS = 6
WIN = 4


def covariance(key, count):
    factor = jax.random.normal(key, (count, count), jnp.float32)
    product = jnp.dot(factor, factor.T, precision=jax.lax.Precision.HIGHEST) / count
    return 0.6 * jnp.eye(count, dtype=jnp.float32) + 0.4 * product


def draw_vertical_cov(key, part):
    return covariance(jax.random.fold_in(key, 11), L).astype(jnp.bfloat16)


def draw_row_cov(key, part):
    return covariance(jax.random.fold_in(key, 23), NY).astype(jnp.bfloat16)


def draw_column_cov(key, part):
    return covariance(jax.random.fold_in(key, 37), NX).astype(jnp.bfloat16)


def block_levels(stream_key, extent, shards, least, high):
    def one(position, parts):
        draws = jax.random.uniform(jax.random.fold_in(jax.random.fold_in(stream_key, 6), position), (parts,), jnp.float32, least / len(shards), high / len(shards))
        return jnp.repeat(jnp.exp(draws), extent[position] // parts).reshape((-1,) + (1,) * (len(extent) - position - 1))

    gain = one(*shards[0])
    for cut in shards[1:]:
        gain = gain * one(*cut)
    return gain


def normal_values(own_key, extent, scale, bound, shards=(), kind=jnp.bfloat16):
    array = jax.random.normal(own_key, extent, jnp.float32) * scale
    if len(shards) > 0:
        array = block_levels(own_key, extent, shards, -0.22, 0.18) * array
    return jnp.clip(array, min=-bound, max=bound).astype(kind)


def setup_inputs(seed: int = 0) -> dict:
    seeds = jax.random.split(jax.random.key(seed), 7)
    return {
        "increment": normal_values(seeds[0], (WIN, L, NY, NX), 1.0, 6.0, ((0, 4), (2, 8)), jnp.float32),
        "diffusivity": jnp.clip(0.04 + 0.16 * jax.random.uniform(seeds[1], (WIN, NY, NX), jnp.float32) ** block_levels(seeds[1], (WIN, NY, NX), ((0, 4), (1, 8)), -0.2, 0.2), 0.04, 0.2),
        "wind": jnp.clip(jax.random.uniform(seeds[2], (WIN, L), jnp.float32, -0.3, 0.3) * block_levels(seeds[2], (WIN, L), ((0, 4),), -0.4, 0.0), -0.3, 0.3),
        "vertical_cov": draw_vertical_cov(jax.random.fold_in(seeds[6], 71), 0),
        "row_cov": draw_row_cov(jax.random.fold_in(seeds[6], 71), 0),
        "column_cov": draw_column_cov(jax.random.fold_in(seeds[6], 71), 0),
    }


VMIX = 0.1


def tendency(center, north, south, kappa, wind_col):
    east = jnp.roll(center, -1, axis=2)
    west = jnp.roll(center, 1, axis=2)
    stacked = jnp.pad(center, ((1, 1), (0, 0), (0, 0)))
    upper = stacked[2:]
    lower = stacked[:-2]
    horiz = north + south + east + west - 4.0 * center
    vert = upper + lower - 2.0 * center
    return center + kappa[None] * horiz + VMIX * vert + wind_col * (0.5 * (south - north))


def reference(increment, diffusivity, wind, vertical_cov, row_cov, column_cov):
    vert_mat = vertical_cov.astype(jnp.float32)
    row_mat = row_cov.astype(jnp.float32)
    col_mat = column_cov.astype(jnp.float32)
    last = increment.shape[0] - 1

    def one(index):
        field = lax.dynamic_index_in_dim(increment, index, 0, keepdims=False)
        kappa = lax.dynamic_index_in_dim(diffusivity, index, 0, keepdims=False)
        wind_col = lax.dynamic_index_in_dim(wind, index, 0, keepdims=False)[:, None, None]
        later = jnp.minimum(index + 1, last).astype(jnp.int32)
        following = lax.dynamic_index_in_dim(increment, later, 0, keepdims=False)
        following = jnp.where(index < last, following, jnp.zeros_like(following))
        current = field
        for step in range(STEPS):
            padded = jnp.pad(current, ((0, 0), (1, 1), (0, 0)))
            current = tendency(current, padded[:, 2:], padded[:, :-2], kappa, wind_col)
        defect = current - following
        levels, height, width = defect.shape
        mixed = jnp.dot(vert_mat, defect.reshape(levels, height * width), precision=lax.Precision.HIGHEST)
        mixed = jnp.dot(mixed.reshape(levels * height, width), col_mat, precision=lax.Precision.HIGHEST)
        mixed = mixed.reshape(levels, height, width)
        return jnp.einsum("yk,zkx->zyx", row_mat, mixed, precision=lax.Precision.HIGHEST)

    return lax.map(one, jnp.arange(increment.shape[0], dtype=jnp.int32))
```

```python
import functools

import jax
import jax.numpy as jnp
from jax import lax
from jax.experimental import pallas as pl
from jax.experimental.pallas import tpu as pltpu
from jax.sharding import PartitionSpec as P

STEPS = 6
VMIX = 0.1
SUB = 8
HALO = STEPS
LANES = 128


F32 = jnp.float32
BF16 = jnp.bfloat16
ANY = pl.BlockSpec(memory_space=pl.ANY)
VM = pl.BlockSpec(memory_space=pltpu.VMEM)
SM = pl.BlockSpec(memory_space=pltpu.SMEM)


def params(limit_mib, sem=None):
    return pltpu.CompilerParams(vmem_limit_bytes=limit_mib << 20, dimension_semantics=sem)


def cost(flops, moved):
    return pl.CostEstimate(flops=int(flops), transcendentals=0, bytes_accessed=int(moved))


def iota(shape, dim):
    return lax.broadcasted_iota(jnp.int32, shape, dim)


def turn(parts):
    parts = list(parts)
    sub = iota(parts[0].shape, 0)
    for d in (4, 2, 1):
        low = (sub & d) == 0
        for i in range(SUB):
            if i & d == 0:
                a, b = parts[i], parts[i + d]
                parts[i] = jnp.where(low, a, pltpu.roll(b, d, axis=0))
                parts[i + d] = jnp.where(low, pltpu.roll(a, SUB - d, axis=0), b)
    return parts


def pieces_kernel(cuts, raw_ref, kap_ref, field_ref, fwd_ref, bwd_ref, *cut_refs):
    step = pl.program_id(0)
    _, per, rows, width = raw_ref.shape
    blocks = per * pl.num_programs(0)
    for p in range(per):
        at = step * per + p
        for tile in range(rows // SUB):
            flat = turn([raw_ref[s, p, tile * SUB : (tile + 1) * SUB, :] for s in range(SUB)])
            for i, part in enumerate(flat):
                row = tile * SUB + i
                field_ref[row, p] = part
                if row < HALO:
                    bwd_ref[row * blocks + at] = part
                if row >= rows - HALO:
                    fwd_ref[(row - rows + HALO) * blocks + at] = part
                for ref, segments in zip(cut_refs, cuts):
                    base = 0
                    for first, count in segments:
                        if first <= row < first + count:
                            ref[base + row - first, p] = part
                        base += count

    @pl.when(step == 0)
    def _():
        fwd_ref[HALO * blocks] = kap_ref[rows - SUB :, :]
        bwd_ref[HALO * blocks] = kap_ref[:SUB, :]


def pieces(raw, kappa, cuts):
    levels, rows, width = raw.shape
    blocks = levels // SUB
    per = 2
    split_raw = raw.reshape(SUB, blocks, rows, width)
    message = jax.ShapeDtypeStruct((HALO * blocks + 1, SUB, width), F32)
    counts = [rows] + [sum(n for _, n in segments) for segments in cuts]
    by_rows = [jax.ShapeDtypeStruct((n, blocks, SUB, width), F32) for n in counts]
    row_specs = [pl.BlockSpec((n, per, SUB, width), lambda i: (0, i, 0, 0)) for n in counts]
    message_spec = pl.BlockSpec(message.shape, lambda i: (0, 0, 0))
    return pl.pallas_call(
        functools.partial(pieces_kernel, cuts),
        name="pieces",
        grid=(blocks // per,),
        in_specs=[
            pl.BlockSpec((SUB, per, rows, width), lambda i: (0, i, 0, 0)),
            pl.BlockSpec((rows, width), lambda i: (0, 0)),
        ],
        out_specs=[row_specs[0]] + [message_spec] * 2 + row_specs[1:],
        out_shape=[by_rows[0]] + [message] * 2 + by_rows[1:],
        compiler_params=params(40),
        cost_estimate=cost(0, 13 * raw.size),
    )(split_raw, kappa)


def steps_kernel(firsts, with_halo, inside_ref, hw_ref, field_ref, kap_ref, *rest):
    if with_halo:
        above_ref, below_ref, out_ref, ping, pong, kap, keep, sem, edge, edge_sem = rest
    else:
        out_ref, ping, pong, kap, keep, sem = rest
    window, _, _, width = ping.shape
    blocks = field_ref.shape[1]
    own = window - HALO if with_halo else window
    seg = pl.program_id(0)
    last = len(firsts) - 1
    first = firsts[0] if last == 0 else jnp.where(seg == 0, firsts[0], firsts[1])
    at = jnp.where(seg == 0, HALO, 0) if with_halo else 0
    edge_at = jnp.where(seg == 0, 0, own) if with_halo else 0
    copy = pltpu.make_async_copy(
        field_ref.at[pl.ds(first, own)], ping.at[pl.ds(at, own), pl.ds(1, blocks)], sem
    )
    copy.start()
    if with_halo:

        @pl.when(seg == 0)
        def _():
            upper = pltpu.make_async_copy(above_ref, edge, edge_sem)
            upper.start()
            upper.wait()

        @pl.when(seg != 0)
        def _():
            lower = pltpu.make_async_copy(below_ref, edge, edge_sem)
            lower.start()
            lower.wait()

    for r in range(own):
        row = jnp.broadcast_to(kap_ref[pl.ds(first + r, 1), :], (SUB, width))
        kap[at + r] = row
        keep[at + r] = (1.0 - 2.0 * VMIX) - 4.0 * row
    sub = iota((SUB, width), 0)
    if with_halo:
        skip = jnp.where(seg == 0, SUB - HALO, 0)
        for r in range(HALO):
            row = jnp.broadcast_to(edge[HALO * blocks, pl.ds(skip + r, 1), :], (SUB, width))
            kap[edge_at + r] = row
            keep[edge_at + r] = (1.0 - 2.0 * VMIX) - 4.0 * row

        def place(r, _):
            ping[edge_at + r, pl.ds(1, blocks)] = edge[pl.ds(r * blocks, blocks)]
            return 0

        lax.fori_loop(0, HALO, place, 0)

    def ghosts(ref, r, first_block, last_block):
        ref[r, 0] = jnp.where(sub == 0, 0.0, pltpu.roll(last_block, 1, axis=0))
        ref[r, blocks + 1] = jnp.where(sub == SUB - 1, 0.0, pltpu.roll(first_block, SUB - 1, axis=0))

    copy.wait()

    def ready(r, _):
        ghosts(ping, r, ping[r, 1], ping[r, blocks])
        return 0

    lax.fori_loop(0, window, ready, 0)

    tiles = width // LANES
    lane = iota((SUB, LANES), 1)
    at_start, at_end = lane == 0, lane == LANES - 1

    def advance(src, dst, r, factor, final):
        def load(row, i):
            return [src[row, i, :, k * LANES : (k + 1) * LANES] for k in range(tiles)]

        before, center = load(r, 0), load(r, 1)
        head = tail = None
        for i in range(1, blocks + 1):
            after, up, down = load(r, i + 1), load(r + 1, i), load(r - 1, i)
            wind = hw_ref[i - 1]
            to_right = [pltpu.roll(c, 1, axis=1) for c in center]
            to_left = [pltpu.roll(c, LANES - 1, axis=1) for c in center]
            new = []
            for k in range(tiles):
                west = jnp.where(at_start, to_right[k - 1], to_right[k])
                east = jnp.where(at_end, to_left[(k + 1) % tiles], to_left[k])
                cols = slice(k * LANES, (k + 1) * LANES)
                value = (
                    keep[r, :, cols] * center[k]
                    + kap[r, :, cols] * ((east + west) + (up[k] + down[k]))
                    + (VMIX * (before[k] + after[k]) + wind * (down[k] - up[k]))
                )
                new.append(value if factor is None else value * factor)
            for k in range(tiles):
                cols = slice(k * LANES, (k + 1) * LANES)
                if final:
                    out_ref[r - HALO, i - 1, :, cols] = new[k]
                else:
                    dst[r, i, :, cols] = new[k]
            head = jnp.concatenate(new, axis=1) if i == 1 else head
            if i == blocks:
                tail = jnp.concatenate(new, axis=1)
            before, center = center, after
        if not final:
            ghosts(dst, r, head, tail)

    refs = (ping, pong)
    for step in range(STEPS):
        src, dst = refs[step % 2], refs[(step + 1) % 2]
        final = step == STEPS - 1
        low, high = step + 1, window - 1 - step

        def body(r, _, src=src, dst=dst, final=final):
            advance(src, dst, r, None, final)
            return 0

        if with_halo and not final:
            inside = inside_ref[seg]

            def masked(r, _, src=src, dst=dst):
                advance(src, dst, r, inside, False)
                return 0

            up_side = seg == 0
            lax.fori_loop(jnp.where(up_side, low, own), jnp.where(up_side, HALO, high), masked, 0)
            lax.fori_loop(jnp.where(up_side, HALO, low), jnp.where(up_side, high, own), body, 0)
        else:
            lax.fori_loop(low, high, body, 0)


def steps(name, firsts, count, inside, half_wind, field, kappa, halos=None):
    _, blocks, _, width = field.shape
    window = count + 2 * HALO
    with_halo = halos is not None
    scratch = [
        pltpu.VMEM((window, blocks + 2, SUB, width), F32),
        pltpu.VMEM((window, blocks + 2, SUB, width), F32),
        pltpu.VMEM((window, SUB, width), F32),
        pltpu.VMEM((window, SUB, width), F32),
        pltpu.SemaphoreType.DMA,
    ]
    if with_halo:
        scratch += [pltpu.VMEM(halos[0].shape, F32), pltpu.SemaphoreType.DMA]
    n = len(firsts)
    updates = n * sum(window - 2 - 2 * s for s in range(STEPS)) * blocks * SUB * width
    return pl.pallas_call(
        functools.partial(steps_kernel, firsts, with_halo),
        name="steps_" + name,
        grid=(n,),
        in_specs=[SM, VM, ANY, VM] + ([ANY, ANY] if with_halo else []),
        out_specs=pl.BlockSpec((count, blocks, SUB, width), lambda i: (i, 0, 0, 0)),
        out_shape=jax.ShapeDtypeStruct((n * count, blocks, SUB, width), F32),
        scratch_shapes=scratch,
        compiler_params=params(40),
        cost_estimate=cost(14 * updates, 4 * n * (window + count) * blocks * SUB * width),
    )(inside, half_wind, field, kappa, *(halos if with_halo else []))


def split(x):
    hi = x.astype(BF16)
    lo = (x - hi.astype(F32)).astype(BF16)
    return hi, lo


def mm(a, b):
    return jnp.dot(a, b, preferred_element_type=F32)


def one_hot(match):
    return match.astype(F32).astype(BF16)


def order_kernel(chunks, devices, me_ref, vert_ref, row_ref, level_ref, *outs):
    levels, rows = vert_ref.shape[0], row_ref.shape[0]
    me = me_ref[0]
    own = levels // devices
    blocks = levels // SUB
    here = rows // devices
    at = iota((levels, levels), 0)
    partner = sum((at >= s * own).astype(jnp.int32) for s in range(1, devices))
    left = one_hot(iota((levels, levels), 1) == (partner ^ me) * own + (at - partner * own))
    at = iota((levels, levels), 1)
    block, sub = at >> (SUB.bit_length() - 1), at & (SUB - 1)
    right = one_hot(iota((levels, levels), 0) == sub * blocks + block)
    level_ref[...] = mm(mm(left, vert_ref[...]).astype(BF16), right).astype(BF16)
    for segments, ref in zip(chunks, outs):
        count = sum(n for _, n in segments)
        at = iota((rows, count * devices), 1)
        partner = sum((at >= s * count).astype(jnp.int32) for s in range(1, devices))
        within = at - partner * count
        source = within + segments[0][0]
        base = 0
        for (first, n), (after, _) in zip(segments, segments[1:]):
            base += n
            source = source + jnp.where(within >= base, after - first - n, 0)
        pick = one_hot(iota((rows, count * devices), 0) == (partner ^ me) * here + source)
        ref[...] = mm(row_ref[...], pick).astype(BF16)


def ordered(chunks, devices, me, vert, row):
    levels, rows = vert.shape[0], row.shape[0]
    widths = [devices * sum(n for _, n in segments) for segments in chunks]
    return pl.pallas_call(
        functools.partial(order_kernel, chunks, devices),
        name="ordered",
        in_specs=[SM, VM, VM],
        out_specs=[VM] * (1 + len(chunks)),
        out_shape=[jax.ShapeDtypeStruct((levels, levels), BF16)]
        + [jax.ShapeDtypeStruct((rows, w), BF16) for w in widths],
        compiler_params=params(16),
        cost_estimate=cost(2 * rows * rows * rows, 4 * rows * rows),
    )(me, vert, row)


def levels_kernel(ev_ref, fo_ref, mat_ref, *outs):
    per, blocks, sub, width = ev_ref.shape
    own = outs[0].shape[1]
    mat = mat_ref[...]
    for r in range(per):
        hi, lo = split((ev_ref[r] - fo_ref[r]).reshape(blocks * sub, width))
        mixed = mm(mat, hi) + mm(mat, lo)
        for s, ref in enumerate(outs):
            ref[r] = mixed[s * own : (s + 1) * own]


def mix_levels(devices, evolved, following, mat):
    rows, blocks, sub, width = evolved.shape
    levels = blocks * sub
    own = levels // devices
    per = 2
    spec = pl.BlockSpec((per, blocks, sub, width), lambda i: (i, 0, 0, 0))
    return pl.pallas_call(
        levels_kernel,
        name="mix_levels",
        grid=(rows // per,),
        in_specs=[spec, spec, pl.BlockSpec(mat.shape, lambda i: (0, 0))],
        out_specs=[pl.BlockSpec((per, own, width), lambda i: (i, 0, 0))] * devices,
        out_shape=[jax.ShapeDtypeStruct((rows, own, width), F32)] * devices,
        compiler_params=params(16),
        cost_estimate=cost(4 * levels * levels * rows * width, 12 * evolved.size),
    )(evolved, following, mat)


def rows_kernel(counts, has_base, col_ref, *rest):
    mats = rest[: len(counts)]
    xs = rest[len(counts) : len(counts) + sum(counts)]
    base_ref = rest[-2] if has_base else None
    out_ref = rest[-1]
    per, _, width = out_ref.shape
    totals = [base_ref[z] if has_base else None for z in range(per)]
    start = 0
    for mat_ref, count in zip(mats, counts):
        x = jnp.concatenate([ref[...] for ref in xs[start : start + count]], axis=0)
        start += count
        depth = x.shape[0]
        hi, lo = split(x.reshape(depth * per, width))
        mixed = (mm(hi, col_ref[...]) + mm(lo, col_ref[...])).reshape(depth, per, width)
        columns = [turn([mixed[g + i] for i in range(SUB)]) for g in range(0, depth, SUB)]
        mat = mat_ref[...]
        for z in range(per):
            hi, lo = split(jnp.concatenate([c[z] for c in columns], axis=0))
            part = mm(mat, hi) + mm(mat, lo)
            totals[z] = part if totals[z] is None else totals[z] + part
    for z in range(per):
        out_ref[z] = totals[z]


def mix_rows(col, mats, groups, base=None):
    blocks = [x for group in groups for x in group]
    own, width = blocks[0].shape[1:]
    rows = mats[0].shape[0]
    has_base = base is not None
    depth = sum(x.shape[0] for x in blocks)
    full = pl.BlockSpec((SUB, rows, width), lambda i: (i, 0, 0))
    whole = [pl.BlockSpec(m.shape, lambda i: (0, 0)) for m in [col, *mats]]
    return pl.pallas_call(
        functools.partial(rows_kernel, [len(g) for g in groups], has_base),
        name="mix_rows",
        grid=(own // SUB,),
        in_specs=whole
        + [pl.BlockSpec((x.shape[0], SUB, width), lambda i: (0, i, 0)) for x in blocks]
        + ([full] if has_base else []),
        out_specs=full,
        out_shape=jax.ShapeDtypeStruct((own, rows, width), F32),
        compiler_params=params(48),
        cost_estimate=cost(
            4 * own * depth * width * (width + rows), 4 * own * width * (depth + rows * (2 if has_base else 1))
        ),
    )(col, *mats, *blocks, *([base] if has_base else []))


def after(x, *others):
    return lax.optimization_barrier((x, *others))[0]


def tiled_body(increment, diffusivity, wind, vertical_cov, row_cov, column_cov):
    raw, kappa = increment[0], diffusivity[0]
    devices, windows = lax.axis_size("tile"), lax.axis_size("win")
    levels, rows, width = raw.shape
    blocks = levels // SUB
    me = lax.axis_index("tile").astype(jnp.int32)
    half_wind = jnp.broadcast_to((0.5 * wind[0]).reshape(SUB, blocks).T[:, :, None], (blocks, SUB, LANES))
    inside = jnp.stack([me != 0, me != devices - 1]).astype(F32)
    middle = rows - 4 * HALO
    chunks = (
        ((2 * HALO, middle),),
        ((HALO, HALO), (rows - 2 * HALO, HALO)),
        ((0, HALO), (rows - HALO, HALO)),
    )
    field, fwd, bwd, *cut = pieces(raw, kappa, chunks)

    def earlier(x):
        return lax.ppermute(x, "win", [(i + 1, i) for i in range(windows - 1)])

    follow = [earlier(cut[0])]
    above = lax.ppermute(fwd, "tile", [(i, i + 1) for i in range(devices - 1)])
    below = lax.ppermute(bwd, "tile", [(i + 1, i) for i in range(devices - 1)])
    follow += [earlier(x) for x in cut[1:]]
    level_mat, *row_mats = ordered(chunks, devices, me.reshape(1), vertical_cov, row_cov)

    def exchange(mixed):
        got = {0: mixed[0]}
        for s in sorted(range(1, devices), key=lambda s: (-(s.bit_length()), s)):
            got[s] = lax.ppermute(mixed[s], "tile", [(t, t ^ s) for t in range(devices)])
        return [got[s] for s in range(devices)]

    ev = steps("middle", [HALO], middle, inside, half_wind, field, kappa)
    mixed = mix_levels(devices, ev, follow[0], level_mat)
    got = [exchange(mixed)]
    ev = steps("inner", [0, rows - 3 * HALO], HALO, inside, half_wind, after(field, mixed[0]), kappa)
    mixed = mix_levels(devices, ev, follow[1], level_mat)
    got.append(exchange(mixed))
    ev = steps("edges", [0, rows - 2 * HALO], HALO, inside, half_wind, after(field, mixed[0]), kappa, [above, below])
    mixed = mix_levels(devices, ev, follow[2], level_mat)
    got.append(exchange(mixed))
    base = mix_rows(column_cov, row_mats[:2], got[:2])
    out = mix_rows(column_cov, row_mats[2:], got[2:], base)
    return out[None]


def with_halo(cells, sides, width):
    for axis, dim in sides:
        count = lax.axis_size(axis)
        ends = count - 1
        head = lax.slice_in_dim(cells, 0, width, axis=dim)
        tail = lax.slice_in_dim(cells, cells.shape[dim] - width, cells.shape[dim], axis=dim)
        cells = jnp.concatenate(
            [
                lax.ppermute(tail, axis, [(i, (i + 1) % count) for i in range(ends)]),
                cells,
                lax.ppermute(head, axis, [((i + 1) % count, i) for i in range(ends)]),
            ],
            axis=dim,
        )
    return cells


def tendency(center, north, south, kappa, wind_col):
    east = jnp.roll(center, -1, axis=2)
    west = jnp.roll(center, 1, axis=2)
    stacked = jnp.pad(center, ((1, 1), (0, 0), (0, 0)))
    horiz = north + south + east + west - 4.0 * center
    vert = stacked[2:] + stacked[:-2] - 2.0 * center
    return center + kappa[None] * horiz + VMIX * vert + wind_col * (0.5 * (south - north))


def plain_body(increment, diffusivity, wind, vertical_cov, row_cov, column_cov):
    field, kappa, wind_col = increment[0], diffusivity[0], wind[0][:, None, None]
    current = field
    for _ in range(STEPS):
        padded = with_halo(current, (("tile", 1),), 1)
        current = tendency(current, padded[:, 2:], padded[:, :-2], kappa, wind_col)
    size = lax.axis_size("win")
    defect = current - lax.ppermute(field, "win", [(i + 1, i) for i in range(size - 1)])
    levels, rows, width = defect.shape
    high = lax.Precision.HIGHEST
    mixed = jnp.dot(vertical_cov.astype(F32), defect.reshape(levels, rows * width), precision=high)
    mixed = jnp.dot(mixed.reshape(levels * rows, width), column_cov.astype(F32), precision=high)
    mixed = lax.all_to_all(mixed.reshape(levels, rows, width), "tile", split_axis=0, concat_axis=1, tiled=True)
    return jnp.einsum("yk,zkx->zyx", row_cov.astype(F32), mixed, precision=high)[None]


def body(*args):
    levels, rows, width = args[0].shape[1:]
    devices = lax.axis_size("tile")
    own = levels // devices
    fits = (
        rows > 4 * HALO
        and rows % SUB == 0
        and levels % (2 * SUB) == 0
        and levels % devices == 0
        and own % SUB == 0
        and width % LANES == 0
        and devices & (devices - 1) == 0
        and devices % SUB == 0
    )
    return tiled_body(*args) if fits else plain_body(*args)


def solution(mesh):
    in_specs = (P("win", None, "tile", None), P("win", "tile", None), P("win", None), P(), P(), P())
    out_specs = P("win", "tile", None, None)
    return jax.shard_map(body, mesh=mesh, in_specs=in_specs, out_specs=out_specs, check_vma=False)
```

```python
import functools

import jax
import jax.numpy as jnp
from jax import lax
from jax.experimental import pallas as pl
from jax.experimental.pallas import tpu as pltpu
from jax.sharding import PartitionSpec as P


STEPS = 6
VMIX = 0.1
SUB = 8
HALO = STEPS
LANES = 128


F32 = jnp.float32
BF16 = jnp.bfloat16
ANY = pl.BlockSpec(memory_space=pl.ANY)
VM = pl.BlockSpec(memory_space=pltpu.VMEM)
SM = pl.BlockSpec(memory_space=pltpu.SMEM)


def params(limit_mib, sem=None):
    return pltpu.CompilerParams(vmem_limit_bytes=limit_mib << 20, dimension_semantics=sem)


def cost(flops, moved):
    return pl.CostEstimate(flops=int(flops), transcendentals=0, bytes_accessed=int(moved))


def iota(shape, dim):
    return lax.broadcasted_iota(jnp.int32, shape, dim)


def turn(parts):
    parts = list(parts)
    sub = iota(parts[0].shape, 0)
    for d in (4, 2, 1):
        low = (sub & d) == 0
        for i in range(SUB):
            if i & d == 0:
                a, b = parts[i], parts[i + d]
                parts[i] = jnp.where(low, a, pltpu.roll(b, d, axis=0))
                parts[i + d] = jnp.where(low, pltpu.roll(a, SUB - d, axis=0), b)
    return parts


def pieces_kernel(me_ref, raw_ref, kap_ref, mid_ref, inner_ref, far_ref, near_ref, buf, sems):
    _, blocks, rows, _ = raw_ref.shape
    parts = sems.shape[0]
    per = blocks // parts
    copies = [
        pltpu.make_async_copy(raw_ref.at[:, pl.ds(i * per, per)], buf.at[:, pl.ds(i * per, per)], sems.at[i])
        for i in range(parts)
    ]
    for c in copies:
        c.start()
    even = (me_ref[0] & 1) == 0

    far_ref[HALO * blocks] = jnp.where(even, kap_ref[:SUB, :], kap_ref[rows - SUB :, :])
    near_ref[HALO * blocks] = jnp.where(even, kap_ref[rows - SUB :, :], kap_ref[:SUB, :])

    def body(at):
        for tile in range(rows // SUB):
            flat = turn([buf[s, at, tile * SUB : (tile + 1) * SUB, :] for s in range(SUB)])
            tops, bottoms = [], []
            for i, part in enumerate(flat):
                row = tile * SUB + i
                if row < HALO:
                    tops.append((row, part))
                elif row < 2 * HALO:
                    inner_ref[(row - HALO) * blocks + at] = part
                elif row < rows - 2 * HALO:
                    mid_ref[(row - 2 * HALO) * blocks + at] = part
                elif row < rows - HALO:
                    inner_ref[(row - rows + 3 * HALO) * blocks + at] = part
                else:
                    bottoms.append((row - rows + HALO, part))
            for is_top, group in ((True, tops), (False, bottoms)):
                if group:

                    @pl.when(even == is_top)
                    def _(group=group):
                        for row, value in group:
                            far_ref[row * blocks + at] = value

                    @pl.when(even != is_top)
                    def _(group=group):
                        for row, value in group:
                            near_ref[row * blocks + at] = value

    for i in range(parts):
        copies[i].wait()

        @pl.loop(i * per, (i + 1) * per)
        def _(at):
            body(at)


def pieces(raw, kappa, me):
    levels, rows, width = raw.shape
    blocks = levels // SUB
    middle = rows - 4 * HALO
    counts = [middle * blocks, 2 * HALO * blocks, HALO * blocks + 1, HALO * blocks + 1]
    return pl.pallas_call(
        pieces_kernel,
        name="pieces",
        in_specs=[SM, pl.BlockSpec(memory_space=pltpu.HBM), VM],
        out_specs=[VM] * 4,
        out_shape=[jax.ShapeDtypeStruct((n, SUB, width), F32) for n in counts],
        scratch_shapes=[pltpu.VMEM((SUB, blocks, rows, width), F32), pltpu.SemaphoreType.DMA((blocks // 2,))],
        compiler_params=params(20),
        cost_estimate=cost(0, 8 * raw.size),
    )(me, raw.reshape(SUB, blocks, rows, width), kappa)


def steps_kernel(plans, firsts, halos, me_ref, inside_ref, hw_ref, kap_ref, *rest):
    extra = 1 if halos else 0
    sources = rest[: len(rest) - 6 - 2 * extra]
    out_ref, ping, pong, kap, keep, sems = rest[len(sources) : len(sources) + 6]
    window, _, _, width = ping.shape
    blocks = ping.shape[1] - 2
    own = window - HALO
    seg = pl.program_id(0)
    even = (me_ref[0] & 1) == 0

    def copies(plan):
        return [
            pltpu.make_async_copy(
                sources[k].at[pl.ds(row * blocks, blocks)], ping.at[to, pl.ds(1, blocks)], sems.at[to]
            )
            for k, row, to in plan
        ]

    def edge_copy(k):
        return pltpu.make_async_copy(sources[k].at[HALO * blocks], rest[-2], rest[-1])

    for (g, parity), (plan, halo) in plans.items():
        here = seg == g if parity is None else (seg == g) & (even == (parity == 0))

        @pl.when(here)
        def _(plan=plan, halo=halo):
            for c in copies(plan):
                c.start()
            if halos:
                edge_copy(halo).start()
                edge_copy(halo).wait()

    def set_rows(r, row):
        row = jnp.broadcast_to(row, (SUB, width))
        kap[r] = row
        keep[r] = (1.0 - 2.0 * VMIX) - 4.0 * row

    first = firsts[0] if len(firsts) == 1 else jnp.where(seg == 0, firsts[0], firsts[1])
    if halos:
        at = jnp.where(seg == 0, HALO, 0)
        for r in range(own):
            set_rows(at + r, kap_ref[pl.ds(first + at + r, 1), :])
        edge_at, skip = jnp.where(seg == 0, 0, own), jnp.where(seg == 0, SUB - HALO, 0)
        for r in range(HALO):
            set_rows(edge_at + r, rest[-2][pl.ds(skip + r, 1), :])
    else:
        for r in range(window):
            set_rows(r, kap_ref[pl.ds(first + r, 1), :])
    sub = iota((SUB, width), 0)
    for (g, parity), (plan, _) in plans.items():
        here = seg == g if parity is None else (seg == g) & (even == (parity == 0))

        @pl.when(here)
        def _(plan=plan):
            for c in copies(plan):
                c.wait()

    def ghosts(ref, r, first_block, last_block):
        ref[r, 0] = jnp.where(sub == 0, 0.0, pltpu.roll(last_block, 1, axis=0))
        ref[r, blocks + 1] = jnp.where(sub == SUB - 1, 0.0, pltpu.roll(first_block, SUB - 1, axis=0))

    def ready(r, _):
        ghosts(ping, r, ping[r, 1], ping[r, blocks])
        return 0

    lax.fori_loop(0, window, ready, 0)

    tiles = width // LANES
    lane = iota((SUB, LANES), 1)
    at_start, at_end = lane == 0, lane == LANES - 1

    def advance(src, dst, r, factor, final):
        def load(row, i):
            return [src[row, i, :, k * LANES : (k + 1) * LANES] for k in range(tiles)]

        before, center = load(r, 0), load(r, 1)
        head = tail = None
        for i in range(1, blocks + 1):
            after, up, down = load(r, i + 1), load(r + 1, i), load(r - 1, i)
            wind = hw_ref[i - 1]
            to_right = [pltpu.roll(c, 1, axis=1) for c in center]
            to_left = [pltpu.roll(c, LANES - 1, axis=1) for c in center]
            new = []
            for k in range(tiles):
                west = jnp.where(at_start, to_right[k - 1], to_right[k])
                east = jnp.where(at_end, to_left[(k + 1) % tiles], to_left[k])
                cols = slice(k * LANES, (k + 1) * LANES)
                value = (
                    keep[r, :, cols] * center[k]
                    + kap[r, :, cols] * ((east + west) + (up[k] + down[k]))
                    + (VMIX * (before[k] + after[k]) + wind * (down[k] - up[k]))
                )
                new.append(value if factor is None else value * factor)
            for k in range(tiles):
                cols = slice(k * LANES, (k + 1) * LANES)
                if final:
                    out_ref[r - HALO, i - 1, :, cols] = new[k]
                else:
                    dst[r, i, :, cols] = new[k]
            head = jnp.concatenate(new, axis=1) if i == 1 else head
            if i == blocks:
                tail = jnp.concatenate(new, axis=1)
            before, center = center, after
        if not final:
            ghosts(dst, r, head, tail)

    refs = (ping, pong)
    for step in range(STEPS):
        src, dst = refs[step % 2], refs[(step + 1) % 2]
        final = step == STEPS - 1
        low, high = step + 1, window - 1 - step

        def body(r, _, src=src, dst=dst, final=final):
            advance(src, dst, r, None, final)
            return 0

        if halos and not final:
            inside = inside_ref[seg]

            def masked(r, _, src=src, dst=dst):
                advance(src, dst, r, inside, False)
                return 0

            up_side = seg == 0
            lax.fori_loop(jnp.where(up_side, low, own), jnp.where(up_side, HALO, high), masked, 0)
            lax.fori_loop(jnp.where(up_side, HALO, low), jnp.where(up_side, high, own), body, 0)
        else:
            lax.fori_loop(low, high, body, 0)


def steps(firsts, count, me, inside, half_wind, kappa, sources, halo_sources=None):
    rows, width = kappa.shape
    blocks = half_wind.shape[0]
    window = count + 2 * HALO
    halos = halo_sources is not None
    arrays = [*sources, *(halo_sources or [])]

    def locate(row, parity):
        if row < 0:
            return (4 if parity == 0 else 5), row + HALO
        if row >= rows:
            return (5 if parity == 0 else 4), row - rows
        if row < HALO:
            return (2 if parity == 0 else 3), row
        if row >= rows - HALO:
            return (3 if parity == 0 else 2), row - rows + HALO
        if row < 2 * HALO:
            return 1, row - HALO
        if row >= rows - 2 * HALO:
            return 1, row - rows + 3 * HALO
        return 0, row - 2 * HALO

    plans = {}
    for g, f in enumerate(firsts):
        for parity in (0, 1):
            plan = [(*locate(f - HALO + r, parity), r) for r in range(window)]
            plans[g, parity] = (plan, (4 if (g == 0) == (parity == 0) else 5))
    used = sorted({k for plan, _ in plans.values() for k, _, _ in plan})
    plans = {
        key: ([(used.index(k), row, to) for k, row, to in plan], used.index(halo) if halos else None)
        for key, (plan, halo) in plans.items()
    }
    n = len(firsts)
    updates = n * sum(window - 2 - 2 * s for s in range(STEPS)) * blocks * SUB * width
    extra = [pltpu.VMEM((SUB, width), F32), pltpu.SemaphoreType.DMA] if halos else []
    return pl.pallas_call(
        functools.partial(steps_kernel, plans, [f - HALO for f in firsts], halos),
        grid=(n,),
        in_specs=[SM, SM, VM, VM] + [ANY] * len(used),
        out_specs=pl.BlockSpec((count, blocks, SUB, width), lambda i: (i, 0, 0, 0)),
        out_shape=jax.ShapeDtypeStruct((n * count, blocks, SUB, width), F32),
        scratch_shapes=[
            pltpu.VMEM((window, blocks + 2, SUB, width), F32),
            pltpu.VMEM((window, blocks + 2, SUB, width), F32),
            pltpu.VMEM((window, SUB, width), F32),
            pltpu.VMEM((window, SUB, width), F32),
            pltpu.SemaphoreType.DMA((window,)),
            *extra,
        ],
        compiler_params=params(24),
        cost_estimate=cost(14 * updates, 4 * n * (window + count) * blocks * SUB * width),
    )(me, inside, half_wind, kappa, *[arrays[k] for k in used])


def split(x):
    hi = x.astype(BF16)
    lo = (x - hi.astype(F32)).astype(BF16)
    return hi, lo


def mm(a, b):
    return jnp.dot(a, b, preferred_element_type=F32)


def one_hot(match):
    return match.astype(F32).astype(BF16)


def order_kernel(chunks, devices, me_ref, vert_ref, row_ref, level_ref, *outs):
    levels, rows = vert_ref.shape[0], row_ref.shape[0]
    me = me_ref[0]
    own = levels // devices
    blocks = levels // SUB
    here = rows // devices
    at = iota((levels, levels), 0)
    partner = sum((at >= s * own).astype(jnp.int32) for s in range(1, devices))
    left = one_hot(iota((levels, levels), 1) == (partner ^ me) * own + (at - partner * own))
    at = iota((levels, levels), 1)
    block, sub = at >> (SUB.bit_length() - 1), at & (SUB - 1)
    right = one_hot(iota((levels, levels), 0) == sub * blocks + block)
    level_ref[...] = mm(mm(left, vert_ref[...]).astype(BF16), right).astype(BF16)
    for segments, ref in zip(chunks, outs):
        count = sum(n for _, n in segments)
        at = iota((rows, 2 * count * devices), 1)
        at = jnp.where(at >= count * devices, at - count * devices, at)
        partner = sum((at >= s * count).astype(jnp.int32) for s in range(1, devices))
        within = at - partner * count
        source = within + segments[0][0]
        base = 0
        for (first, n), (after, _) in zip(segments, segments[1:]):
            base += n
            source = source + jnp.where(within >= base, after - first - n, 0)
        pick = one_hot(iota((rows, 2 * count * devices), 0) == (partner ^ me) * here + source)
        ref[...] = mm(row_ref[...], pick).astype(BF16)


def ordered(chunks, devices, me, vert, row):
    levels, rows = vert.shape[0], row.shape[0]
    widths = [2 * devices * sum(n for _, n in segments) for segments in chunks]
    return pl.pallas_call(
        functools.partial(order_kernel, chunks, devices),
        name="ordered",
        in_specs=[SM, VM, VM],
        out_specs=[VM] * (1 + len(chunks)),
        out_shape=[jax.ShapeDtypeStruct((levels, levels), BF16)]
        + [jax.ShapeDtypeStruct((rows, w), BF16) for w in widths],
        compiler_params=params(16),
        cost_estimate=cost(2 * rows * rows * rows, 4 * rows * rows),
    )(me, vert, row)


def levels_kernel(edges, with_columns, me_ref, ev_ref, mat_ref, *rest):
    fo_refs, rest = rest[: 2 if edges else 1], rest[2 if edges else 1 :]
    col_ref, outs = (rest[0], rest[1:]) if with_columns else (None, rest)
    per, blocks, sub, width = ev_ref.shape
    own = outs[0].shape[1]
    late = (pl.program_id(0) >= pl.num_programs(0) // 2).astype(jnp.int32)
    near = late != (me_ref[0] & 1)
    mat = mat_ref[...]
    for r in range(per):
        following = fo_refs[0][r * blocks : (r + 1) * blocks]
        if edges:
            following = jnp.where(near, fo_refs[1][r * blocks : (r + 1) * blocks], following)
        hi, lo = split((ev_ref[r] - following).reshape(blocks * sub, width))
        mixed = mm(mat, hi) + mm(mat, lo)
        if with_columns:
            hi, lo = split(mixed)
            mixed = mm(hi, col_ref[...]) + mm(lo, col_ref[...])
        for s, ref in enumerate(outs):
            ref[r] = mixed[s * own : (s + 1) * own]


def mix_levels(count, me, evolved, following, mat, col=None):
    rows, blocks, sub, width = evolved.shape
    levels = blocks * sub
    own = levels // count
    per = 2
    edges = len(following) == 2
    half = rows // (2 * per)
    spec = pl.BlockSpec((per * blocks, sub, width), lambda i: (lax.rem(i, half) if edges else i, 0, 0))
    cols = [] if col is None else [col]
    return pl.pallas_call(
        functools.partial(levels_kernel, edges, col is not None),
        name="mix_levels",
        grid=(rows // per,),
        in_specs=[
            SM,
            pl.BlockSpec((per, blocks, sub, width), lambda i: (i, 0, 0, 0)),
            pl.BlockSpec(mat.shape, lambda i: (0, 0)),
        ]
        + [spec] * len(following)
        + [pl.BlockSpec(c.shape, lambda i: (0, 0)) for c in cols],
        out_specs=[pl.BlockSpec((per, own, width), lambda i: (i, 0, 0))] * count,
        out_shape=[jax.ShapeDtypeStruct((rows, own, width), F32)] * count,
        compiler_params=params(16),
        cost_estimate=cost(4 * levels * levels * rows * width, 12 * evolved.size),
    )(me, evolved, mat, *following, *cols)


def by_level(x):
    groups = [turn([x[g + i] for i in range(SUB)]) for g in range(0, x.shape[0], SUB)]
    return [jnp.concatenate([g[z] for g in groups], axis=0) for z in range(SUB)]


def stacked(x):
    return jnp.concatenate(split(x), axis=0)


def rows_kernel(counts, col_ref, *rest):
    mats, xs, out_ref = rest[: len(counts)], rest[len(counts) : -1], rest[-1]
    width = out_ref.shape[2]
    totals = [None] * SUB
    start = 0
    for mat_ref, count in zip(mats, counts):
        x = jnp.concatenate([ref[...] for ref in xs[start : start + count]], axis=0)
        start += count
        depth = x.shape[0]
        hi, lo = split(x.reshape(depth * SUB, width))
        mixed = (mm(hi, col_ref[...]) + mm(lo, col_ref[...])).reshape(depth, SUB, width)
        for z, level in enumerate(by_level(mixed)):
            part = mm(mat_ref[...], stacked(level))
            totals[z] = part if totals[z] is None else totals[z] + part
    for z in range(SUB):
        out_ref[z] = totals[z]


def mix_rows(col, mats, groups):
    blocks = [x for group in groups for x in group]
    own, width = blocks[0].shape[1:]
    rows = mats[0].shape[0]
    depth = sum(x.shape[0] for x in blocks)
    return pl.pallas_call(
        functools.partial(rows_kernel, [len(g) for g in groups]),
        name="mix_rows",
        grid=(own // SUB,),
        in_specs=[pl.BlockSpec(m.shape, lambda i: (0, 0)) for m in [col, *mats]]
        + [pl.BlockSpec((x.shape[0], SUB, width), lambda i: (0, i, 0)) for x in blocks],
        out_specs=pl.BlockSpec((SUB, rows, width), lambda i: (i, 0, 0)),
        out_shape=jax.ShapeDtypeStruct((own, rows, width), F32),
        compiler_params=params(36),
        cost_estimate=cost(4 * own * depth * width * (width + rows), 4 * own * width * (depth + rows)),
    )(col, *mats, *blocks)


def finish_kernel(count, mat_ref, base_ref, *rest):
    out_ref = rest[-1]
    x = jnp.concatenate([ref[...] for ref in rest[:count]], axis=0)
    for z, level in enumerate(by_level(x)):
        out_ref[z] = base_ref[z] + mm(mat_ref[...], stacked(level))


def finish(part, mat, base, blocks, out=None):
    _, rows, width = base.shape
    cols = LANES
    spec = pl.BlockSpec((SUB, rows, cols), lambda j: (part, 0, j))
    rest = [] if out is None else [out]
    depth = sum(x.shape[0] for x in blocks)
    return pl.pallas_call(
        functools.partial(finish_kernel, len(blocks)),
        name="finish",
        grid=(width // cols,),
        in_specs=[pl.BlockSpec(mat.shape, lambda j: (0, 0)), spec]
        + [pl.BlockSpec((x.shape[0], SUB, cols), lambda j: (0, 0, j)) for x in blocks]
        + [ANY] * len(rest),
        out_specs=spec,
        out_shape=jax.ShapeDtypeStruct(base.shape, F32),
        input_output_aliases={2 + len(blocks): 0} if rest else {},
        compiler_params=params(16),
        cost_estimate=cost(4 * SUB * depth * rows * width, 4 * SUB * width * (depth + 2 * rows)),
    )(mat, base, *blocks, *rest)


def tiled_body(increment, diffusivity, wind, vertical_cov, row_cov, column_cov):
    raw, kappa = increment[0], diffusivity[0]
    devices, windows = lax.axis_size("tile"), lax.axis_size("win")
    levels, rows, _ = raw.shape
    blocks = levels // SUB
    me = lax.axis_index("tile").astype(jnp.int32)
    half_wind = jnp.broadcast_to((0.5 * wind[0]).reshape(SUB, blocks).T[:, :, None], (blocks, SUB, LANES))
    inside = jnp.stack([me != 0, me != devices - 1]).astype(F32)
    middle = rows - 4 * HALO
    chunks = (
        ((2 * HALO, middle),),
        ((HALO, HALO), (rows - 2 * HALO, HALO)),
        ((0, HALO), (rows - HALO, HALO)),
    )
    one = me.reshape(1)
    mids, inner, far, near = pieces(raw, kappa, one)

    def earlier(x):
        return lax.ppermute(x, "win", [(i + 1, i) for i in range(windows - 1)])

    apart = [(t, t + 1) for t in range(1, devices - 1, 2)] + [(t + 1, t) for t in range(1, devices - 1, 2)]
    far_in = lax.ppermute(far, "tile", apart)
    follow_mids = earlier(mids)
    near_in = lax.ppermute(near, "tile", [(t, t ^ 1) for t in range(devices)])
    level_mat, *row_mats = ordered(chunks, devices, one, vertical_cov, row_cov)

    def exchange(parts):
        got = {}
        for s in sorted(range(1, devices), key=lambda s: (-(s.bit_length()), s)):
            got[s] = lax.ppermute(parts[s], "tile", [(t, t ^ s) for t in range(devices)])
        return [parts[0]] + [got[s] for s in range(1, devices)]

    own = [mids, inner, far, near]
    ev = steps([2 * HALO], middle, one, inside, half_wind, kappa, own)
    mixed = mix_levels(devices, one, ev, [follow_mids], level_mat)
    first = exchange(mixed)

    *own, _ = lax.optimization_barrier((mids, inner, far, near, mixed[0]))
    follow_inner, follow_far, follow_near = earlier(own[1]), earlier(own[2]), earlier(own[3])
    ev = steps([HALO, rows - 2 * HALO], HALO, one, inside, half_wind, kappa, own)
    mixed = mix_levels(devices, one, ev, [follow_inner], level_mat)
    second = exchange(mixed)

    *own, _ = lax.optimization_barrier((*own, mixed[0]))
    ev = steps([0, rows - HALO], HALO, one, inside, half_wind, kappa, own, [far_in, near_in])
    halves = levels // devices // SUB
    mixed = mix_levels(devices * halves, one, ev, [follow_far, follow_near], level_mat, column_cov)
    base = mix_rows(column_cov, row_mats[:2], [first, second])
    out = None
    for h in range(halves):
        last = exchange(mixed[h::halves])
        out = finish(h, row_mats[2], base, last, out)
    return out[None]


def with_halo(cells, sides, width):
    for axis, dim in sides:
        count = lax.axis_size(axis)
        ends = count - 1
        head = lax.slice_in_dim(cells, 0, width, axis=dim)
        tail = lax.slice_in_dim(cells, cells.shape[dim] - width, cells.shape[dim], axis=dim)
        cells = jnp.concatenate(
            [
                lax.ppermute(tail, axis, [(i, (i + 1) % count) for i in range(ends)]),
                cells,
                lax.ppermute(head, axis, [((i + 1) % count, i) for i in range(ends)]),
            ],
            axis=dim,
        )
    return cells


def tendency(center, north, south, kappa, wind_col):
    east = jnp.roll(center, -1, axis=2)
    west = jnp.roll(center, 1, axis=2)
    stacked = jnp.pad(center, ((1, 1), (0, 0), (0, 0)))
    horiz = north + south + east + west - 4.0 * center
    vert = stacked[2:] + stacked[:-2] - 2.0 * center
    return center + kappa[None] * horiz + VMIX * vert + wind_col * (0.5 * (south - north))


def plain_body(increment, diffusivity, wind, vertical_cov, row_cov, column_cov):
    field, kappa, wind_col = increment[0], diffusivity[0], wind[0][:, None, None]
    current = field
    for _ in range(STEPS):
        padded = with_halo(current, (("tile", 1),), 1)
        current = tendency(current, padded[:, 2:], padded[:, :-2], kappa, wind_col)
    size = lax.axis_size("win")
    defect = current - lax.ppermute(field, "win", [(i + 1, i) for i in range(size - 1)])
    levels, rows, width = defect.shape
    high = lax.Precision.HIGHEST
    mixed = jnp.dot(vertical_cov.astype(F32), defect.reshape(levels, rows * width), precision=high)
    mixed = jnp.dot(mixed.reshape(levels * rows, width), column_cov.astype(F32), precision=high)
    mixed = lax.all_to_all(mixed.reshape(levels, rows, width), "tile", split_axis=0, concat_axis=1, tiled=True)
    return jnp.einsum("yk,zkx->zyx", row_cov.astype(F32), mixed, precision=high)[None]


def body(*args):
    levels, rows, width = args[0].shape[1:]
    devices = lax.axis_size("tile")
    own = levels // devices
    fits = (
        rows > 4 * HALO
        and rows % SUB == 0
        and levels % (2 * SUB) == 0
        and levels % devices == 0
        and own % SUB == 0
        and width % LANES == 0
        and devices & (devices - 1) == 0
        and devices % SUB == 0
    )
    return tiled_body(*args) if fits else plain_body(*args)


def solution(mesh):
    in_specs = (P("win", None, "tile", None), P("win", "tile", None), P("win", None), P(), P(), P())
    out_specs = P("win", "tile", None, None)
    return jax.shard_map(body, mesh=mesh, in_specs=in_specs, out_specs=out_specs, check_vma=False)
```

```python
import functools

import jax
import jax.numpy as jnp
from jax import lax
from jax.experimental import pallas as pl
from jax.experimental.pallas import tpu as pltpu
from jax.sharding import PartitionSpec as P


STEPS = 6
VMIX = 0.1
SUB = 8
HALO = STEPS
LANES = 128


F32 = jnp.float32
BF16 = jnp.bfloat16
ANY = pl.BlockSpec(memory_space=pl.ANY)
VM = pl.BlockSpec(memory_space=pltpu.VMEM)
SM = pl.BlockSpec(memory_space=pltpu.SMEM)


def params(limit_mib, sem=None):
    return pltpu.CompilerParams(vmem_limit_bytes=limit_mib << 20, dimension_semantics=sem)


def cost(flops, moved):
    return pl.CostEstimate(flops=int(flops), transcendentals=0, bytes_accessed=int(moved))


def iota(shape, dim):
    return lax.broadcasted_iota(jnp.int32, shape, dim)


def turn(parts):
    parts = list(parts)
    sub = iota(parts[0].shape, 0)
    for d in (4, 2, 1):
        low = (sub & d) == 0
        for i in range(SUB):
            if i & d == 0:
                a, b = parts[i], parts[i + d]
                parts[i] = jnp.where(low, a, pltpu.roll(b, d, axis=0))
                parts[i + d] = jnp.where(low, pltpu.roll(a, SUB - d, axis=0), b)
    return parts


def pieces_kernel(me_ref, raw_ref, kap_ref, mid_ref, inner_ref, far_ref, near_ref):
    _, blocks, rows, _ = raw_ref.shape
    even = (me_ref[0] & 1) == 0

    far_ref[HALO * blocks] = jnp.where(even, kap_ref[:SUB, :], kap_ref[rows - SUB :, :])
    near_ref[HALO * blocks] = jnp.where(even, kap_ref[rows - SUB :, :], kap_ref[:SUB, :])

    def body(at):
        for tile in range(rows // SUB):
            flat = turn([raw_ref[s, at, tile * SUB : (tile + 1) * SUB, :] for s in range(SUB)])
            tops, bottoms = [], []
            for i, part in enumerate(flat):
                row = tile * SUB + i
                if row < HALO:
                    tops.append((row, part))
                elif row < 2 * HALO:
                    inner_ref[(row - HALO) * blocks + at] = part
                elif row < rows - 2 * HALO:
                    mid_ref[(row - 2 * HALO) * blocks + at] = part
                elif row < rows - HALO:
                    inner_ref[(row - rows + 3 * HALO) * blocks + at] = part
                else:
                    bottoms.append((row - rows + HALO, part))
            for is_top, group in ((True, tops), (False, bottoms)):
                if group:

                    @pl.when(even == is_top)
                    def _(group=group):
                        for row, value in group:
                            far_ref[row * blocks + at] = value

                    @pl.when(even != is_top)
                    def _(group=group):
                        for row, value in group:
                            near_ref[row * blocks + at] = value

    @pl.loop(0, blocks)
    def _(at):
        body(at)


def pieces(raw, kappa, me):
    levels, rows, width = raw.shape
    blocks = levels // SUB
    middle = rows - 4 * HALO
    counts = [middle * blocks, 2 * HALO * blocks, HALO * blocks + 1, HALO * blocks + 1]
    return pl.pallas_call(
        pieces_kernel,
        name="pieces",
        in_specs=[SM, VM, VM],
        out_specs=[VM] * 4,
        out_shape=[jax.ShapeDtypeStruct((n, SUB, width), F32) for n in counts],
        compiler_params=params(20),
        cost_estimate=cost(0, 8 * raw.size),
    )(me, raw.reshape(SUB, blocks, rows, width), kappa)


def steps_kernel(plans, firsts, halos, me_ref, inside_ref, hw_ref, kap_ref, *rest):
    extra = 1 if halos else 0
    sources = rest[: len(rest) - 6 - 2 * extra]
    out_ref, ping, pong, kap, keep, sems = rest[len(sources) : len(sources) + 6]
    window, _, _, width = ping.shape
    blocks = ping.shape[1] - 2
    own = window - HALO
    seg = pl.program_id(0)
    even = (me_ref[0] & 1) == 0

    def copies(plan):
        return [
            pltpu.make_async_copy(
                sources[k].at[pl.ds(row * blocks, blocks)], ping.at[to, pl.ds(1, blocks)], sems.at[to]
            )
            for k, row, to in plan
        ]

    def edge_copy(k):
        return pltpu.make_async_copy(sources[k].at[HALO * blocks], rest[-2], rest[-1])

    for (g, parity), (plan, halo) in plans.items():
        here = seg == g if parity is None else (seg == g) & (even == (parity == 0))

        @pl.when(here)
        def _(plan=plan, halo=halo):
            for c in copies(plan):
                c.start()
            if halos:
                edge_copy(halo).start()
                edge_copy(halo).wait()

    def set_rows(r, row):
        row = jnp.broadcast_to(row, (SUB, width))
        kap[r] = row
        keep[r] = (1.0 - 2.0 * VMIX) - 4.0 * row

    first = firsts[0] if len(firsts) == 1 else jnp.where(seg == 0, firsts[0], firsts[1])
    if halos:
        at = jnp.where(seg == 0, HALO, 0)
        for r in range(own):
            set_rows(at + r, kap_ref[pl.ds(first + at + r, 1), :])
        edge_at, skip = jnp.where(seg == 0, 0, own), jnp.where(seg == 0, SUB - HALO, 0)
        for r in range(HALO):
            set_rows(edge_at + r, rest[-2][pl.ds(skip + r, 1), :])
    else:
        for r in range(window):
            set_rows(r, kap_ref[pl.ds(first + r, 1), :])
    sub = iota((SUB, width), 0)
    for (g, parity), (plan, _) in plans.items():
        here = seg == g if parity is None else (seg == g) & (even == (parity == 0))

        @pl.when(here)
        def _(plan=plan):
            for c in copies(plan):
                c.wait()

    def ghosts(ref, r, first_block, last_block):
        ref[r, 0] = jnp.where(sub == 0, 0.0, pltpu.roll(last_block, 1, axis=0))
        ref[r, blocks + 1] = jnp.where(sub == SUB - 1, 0.0, pltpu.roll(first_block, SUB - 1, axis=0))

    def ready(r, _):
        ghosts(ping, r, ping[r, 1], ping[r, blocks])
        return 0

    lax.fori_loop(0, window, ready, 0)

    tiles = width // LANES
    lane = iota((SUB, LANES), 1)
    at_start, at_end = lane == 0, lane == LANES - 1

    def advance(src, dst, r, factor, final):
        def load(row, i):
            return [src[row, i, :, k * LANES : (k + 1) * LANES] for k in range(tiles)]

        before, center = load(r, 0), load(r, 1)
        head = tail = None
        for i in range(1, blocks + 1):
            after, up, down = load(r, i + 1), load(r + 1, i), load(r - 1, i)
            wind = hw_ref[i - 1]
            to_right = [pltpu.roll(c, 1, axis=1) for c in center]
            to_left = [pltpu.roll(c, LANES - 1, axis=1) for c in center]
            new = []
            for k in range(tiles):
                west = jnp.where(at_start, to_right[k - 1], to_right[k])
                east = jnp.where(at_end, to_left[(k + 1) % tiles], to_left[k])
                cols = slice(k * LANES, (k + 1) * LANES)
                value = (
                    keep[r, :, cols] * center[k]
                    + kap[r, :, cols] * ((east + west) + (up[k] + down[k]))
                    + (VMIX * (before[k] + after[k]) + wind * (down[k] - up[k]))
                )
                new.append(value if factor is None else value * factor)
            for k in range(tiles):
                cols = slice(k * LANES, (k + 1) * LANES)
                if final:
                    out_ref[r - HALO, i - 1, :, cols] = new[k]
                else:
                    dst[r, i, :, cols] = new[k]
            head = jnp.concatenate(new, axis=1) if i == 1 else head
            if i == blocks:
                tail = jnp.concatenate(new, axis=1)
            before, center = center, after
        if not final:
            ghosts(dst, r, head, tail)

    refs = (ping, pong)
    for step in range(STEPS):
        src, dst = refs[step % 2], refs[(step + 1) % 2]
        final = step == STEPS - 1
        low, high = step + 1, window - 1 - step

        def body(r, _, src=src, dst=dst, final=final):
            advance(src, dst, r, None, final)
            return 0

        if halos and not final:
            inside = inside_ref[seg]

            def masked(r, _, src=src, dst=dst):
                advance(src, dst, r, inside, False)
                return 0

            up_side = seg == 0
            lax.fori_loop(jnp.where(up_side, low, own), jnp.where(up_side, HALO, high), masked, 0)
            lax.fori_loop(jnp.where(up_side, HALO, low), jnp.where(up_side, high, own), body, 0)
        else:
            lax.fori_loop(low, high, body, 0)


def steps(firsts, count, me, inside, half_wind, kappa, sources, halo_sources=None):
    rows, width = kappa.shape
    blocks = half_wind.shape[0]
    window = count + 2 * HALO
    halos = halo_sources is not None
    arrays = [*sources, *(halo_sources or [])]

    def locate(row, parity):
        if row < 0:
            return (4 if parity == 0 else 5), row + HALO
        if row >= rows:
            return (5 if parity == 0 else 4), row - rows
        if row < HALO:
            return (2 if parity == 0 else 3), row
        if row >= rows - HALO:
            return (3 if parity == 0 else 2), row - rows + HALO
        if row < 2 * HALO:
            return 1, row - HALO
        if row >= rows - 2 * HALO:
            return 1, row - rows + 3 * HALO
        return 0, row - 2 * HALO

    plans = {}
    for g, f in enumerate(firsts):
        for parity in (0, 1):
            plan = [(*locate(f - HALO + r, parity), r) for r in range(window)]
            plans[g, parity] = (plan, (4 if (g == 0) == (parity == 0) else 5))
    used = sorted({k for plan, _ in plans.values() for k, _, _ in plan})
    plans = {
        key: ([(used.index(k), row, to) for k, row, to in plan], used.index(halo) if halos else None)
        for key, (plan, halo) in plans.items()
    }
    n = len(firsts)
    updates = n * sum(window - 2 - 2 * s for s in range(STEPS)) * blocks * SUB * width
    extra = [pltpu.VMEM((SUB, width), F32), pltpu.SemaphoreType.DMA] if halos else []
    return pl.pallas_call(
        functools.partial(steps_kernel, plans, [f - HALO for f in firsts], halos),
        grid=(n,),
        in_specs=[SM, SM, VM, VM] + [ANY] * len(used),
        out_specs=pl.BlockSpec((count, blocks, SUB, width), lambda i: (i, 0, 0, 0)),
        out_shape=jax.ShapeDtypeStruct((n * count, blocks, SUB, width), F32),
        scratch_shapes=[
            pltpu.VMEM((window, blocks + 2, SUB, width), F32),
            pltpu.VMEM((window, blocks + 2, SUB, width), F32),
            pltpu.VMEM((window, SUB, width), F32),
            pltpu.VMEM((window, SUB, width), F32),
            pltpu.SemaphoreType.DMA((window,)),
            *extra,
        ],
        compiler_params=params(24),
        cost_estimate=cost(14 * updates, 4 * n * (window + count) * blocks * SUB * width),
    )(me, inside, half_wind, kappa, *[arrays[k] for k in used])


def split(x):
    hi = x.astype(BF16)
    lo = (x - hi.astype(F32)).astype(BF16)
    return hi, lo


def mm(a, b):
    return jnp.dot(a, b, preferred_element_type=F32)


def one_hot(match):
    return match.astype(F32).astype(BF16)


def order_kernel(chunks, devices, me_ref, vert_ref, row_ref, level_ref, *outs):
    levels, rows = vert_ref.shape[0], row_ref.shape[0]
    me = me_ref[0]
    own = levels // devices
    blocks = levels // SUB
    here = rows // devices
    at = iota((levels, levels), 0)
    partner = sum((at >= s * own).astype(jnp.int32) for s in range(1, devices))
    left = one_hot(iota((levels, levels), 1) == (partner ^ me) * own + (at - partner * own))
    at = iota((levels, levels), 1)
    block, sub = at >> (SUB.bit_length() - 1), at & (SUB - 1)
    right = one_hot(iota((levels, levels), 0) == sub * blocks + block)
    level_ref[...] = mm(mm(left, vert_ref[...]).astype(BF16), right).astype(BF16)
    for segments, ref in zip(chunks, outs):
        count = sum(n for _, n in segments)
        at = iota((rows, 2 * count * devices), 1)
        at = jnp.where(at >= count * devices, at - count * devices, at)
        partner = sum((at >= s * count).astype(jnp.int32) for s in range(1, devices))
        within = at - partner * count
        source = within + segments[0][0]
        base = 0
        for (first, n), (after, _) in zip(segments, segments[1:]):
            base += n
            source = source + jnp.where(within >= base, after - first - n, 0)
        pick = one_hot(iota((rows, 2 * count * devices), 0) == (partner ^ me) * here + source)
        ref[...] = mm(row_ref[...], pick).astype(BF16)


def ordered(chunks, devices, me, vert, row):
    levels, rows = vert.shape[0], row.shape[0]
    widths = [2 * devices * sum(n for _, n in segments) for segments in chunks]
    return pl.pallas_call(
        functools.partial(order_kernel, chunks, devices),
        name="ordered",
        in_specs=[SM, VM, VM],
        out_specs=[VM] * (1 + len(chunks)),
        out_shape=[jax.ShapeDtypeStruct((levels, levels), BF16)]
        + [jax.ShapeDtypeStruct((rows, w), BF16) for w in widths],
        compiler_params=params(16),
        cost_estimate=cost(2 * rows * rows * rows, 4 * rows * rows),
    )(me, vert, row)


def levels_kernel(edges, with_columns, me_ref, ev_ref, mat_ref, *rest):
    fo_refs, rest = rest[: 2 if edges else 1], rest[2 if edges else 1 :]
    col_ref, outs = (rest[0], rest[1:]) if with_columns else (None, rest)
    per, blocks, sub, width = ev_ref.shape
    own = outs[0].shape[1]
    late = (pl.program_id(0) >= pl.num_programs(0) // 2).astype(jnp.int32)
    near = late != (me_ref[0] & 1)
    mat = mat_ref[...]
    for r in range(per):
        following = fo_refs[0][r * blocks : (r + 1) * blocks]
        if edges:
            following = jnp.where(near, fo_refs[1][r * blocks : (r + 1) * blocks], following)
        hi, lo = split((ev_ref[r] - following).reshape(blocks * sub, width))
        mixed = mm(mat, hi) + mm(mat, lo)
        if with_columns:
            hi, lo = split(mixed)
            mixed = mm(hi, col_ref[...]) + mm(lo, col_ref[...])
        for s, ref in enumerate(outs):
            ref[r] = mixed[s * own : (s + 1) * own]


def mix_levels(count, me, evolved, following, mat, col=None):
    rows, blocks, sub, width = evolved.shape
    levels = blocks * sub
    own = levels // count
    per = 2
    edges = len(following) == 2
    half = rows // (2 * per)
    spec = pl.BlockSpec((per * blocks, sub, width), lambda i: (lax.rem(i, half) if edges else i, 0, 0))
    cols = [] if col is None else [col]
    return pl.pallas_call(
        functools.partial(levels_kernel, edges, col is not None),
        name="mix_levels",
        grid=(rows // per,),
        in_specs=[
            SM,
            pl.BlockSpec((per, blocks, sub, width), lambda i: (i, 0, 0, 0)),
            pl.BlockSpec(mat.shape, lambda i: (0, 0)),
        ]
        + [spec] * len(following)
        + [pl.BlockSpec(c.shape, lambda i: (0, 0)) for c in cols],
        out_specs=[pl.BlockSpec((per, own, width), lambda i: (i, 0, 0))] * count,
        out_shape=[jax.ShapeDtypeStruct((rows, own, width), F32)] * count,
        compiler_params=params(16),
        cost_estimate=cost(4 * levels * levels * rows * width, 12 * evolved.size),
    )(me, evolved, mat, *following, *cols)


def by_level(x):
    groups = [turn([x[g + i] for i in range(SUB)]) for g in range(0, x.shape[0], SUB)]
    return [jnp.concatenate([g[z] for g in groups], axis=0) for z in range(SUB)]


def stacked(x):
    return jnp.concatenate(split(x), axis=0)


def rows_kernel(counts, col_ref, *rest):
    mats, xs, out_ref = rest[: len(counts)], rest[len(counts) : -1], rest[-1]
    width = out_ref.shape[2]
    totals = [None] * SUB
    start = 0
    for mat_ref, count in zip(mats, counts):
        x = jnp.concatenate([ref[...] for ref in xs[start : start + count]], axis=0)
        start += count
        depth = x.shape[0]
        hi, lo = split(x.reshape(depth * SUB, width))
        mixed = (mm(hi, col_ref[...]) + mm(lo, col_ref[...])).reshape(depth, SUB, width)
        for z, level in enumerate(by_level(mixed)):
            part = mm(mat_ref[...], stacked(level))
            totals[z] = part if totals[z] is None else totals[z] + part
    for z in range(SUB):
        out_ref[z] = totals[z]


def mix_rows(col, mats, groups):
    blocks = [x for group in groups for x in group]
    own, width = blocks[0].shape[1:]
    rows = mats[0].shape[0]
    depth = sum(x.shape[0] for x in blocks)
    return pl.pallas_call(
        functools.partial(rows_kernel, [len(g) for g in groups]),
        name="mix_rows",
        grid=(own // SUB,),
        in_specs=[pl.BlockSpec(m.shape, lambda i: (0, 0)) for m in [col, *mats]]
        + [pl.BlockSpec((x.shape[0], SUB, width), lambda i: (0, i, 0)) for x in blocks],
        out_specs=pl.BlockSpec((SUB, rows, width), lambda i: (i, 0, 0)),
        out_shape=jax.ShapeDtypeStruct((own, rows, width), F32),
        compiler_params=params(36),
        cost_estimate=cost(4 * own * depth * width * (width + rows), 4 * own * width * (depth + rows)),
    )(col, *mats, *blocks)


def finish_kernel(count, mat_ref, base_ref, *rest):
    out_ref = rest[-1]
    x = jnp.concatenate([ref[...] for ref in rest[:count]], axis=0)
    for z, level in enumerate(by_level(x)):
        out_ref[z] = base_ref[z] + mm(mat_ref[...], stacked(level))


def finish(part, mat, base, blocks, out=None):
    _, rows, width = base.shape
    cols = 2 * LANES if width % (2 * LANES) == 0 else LANES
    spec = pl.BlockSpec((SUB, rows, cols), lambda j: (part, 0, j))
    rest = [] if out is None else [out]
    depth = sum(x.shape[0] for x in blocks)
    return pl.pallas_call(
        functools.partial(finish_kernel, len(blocks)),
        name="finish",
        grid=(width // cols,),
        in_specs=[pl.BlockSpec(mat.shape, lambda j: (0, 0)), spec]
        + [pl.BlockSpec((x.shape[0], SUB, cols), lambda j: (0, 0, j)) for x in blocks]
        + [ANY] * len(rest),
        out_specs=spec,
        out_shape=jax.ShapeDtypeStruct(base.shape, F32),
        input_output_aliases={2 + len(blocks): 0} if rest else {},
        compiler_params=params(16),
        cost_estimate=cost(4 * SUB * depth * rows * width, 4 * SUB * width * (depth + 2 * rows)),
    )(mat, base, *blocks, *rest)


def tiled_body(increment, diffusivity, wind, vertical_cov, row_cov, column_cov):
    raw, kappa = increment[0], diffusivity[0]
    devices, windows = lax.axis_size("tile"), lax.axis_size("win")
    levels, rows, _ = raw.shape
    blocks = levels // SUB
    me = lax.axis_index("tile").astype(jnp.int32)
    half_wind = jnp.broadcast_to((0.5 * wind[0]).reshape(SUB, blocks).T[:, :, None], (blocks, SUB, LANES))
    inside = jnp.stack([me != 0, me != devices - 1]).astype(F32)
    middle = rows - 4 * HALO
    chunks = (
        ((2 * HALO, middle),),
        ((HALO, HALO), (rows - 2 * HALO, HALO)),
        ((0, HALO), (rows - HALO, HALO)),
    )
    one = me.reshape(1)
    mids, inner, far, near = pieces(raw, kappa, one)

    def earlier(x):
        return lax.ppermute(x, "win", [(i + 1, i) for i in range(windows - 1)])

    apart = [(t, t + 1) for t in range(1, devices - 1, 2)] + [(t + 1, t) for t in range(1, devices - 1, 2)]
    far_in = lax.ppermute(far, "tile", apart)
    follow_mids = earlier(mids)
    near_in = lax.ppermute(near, "tile", [(t, t ^ 1) for t in range(devices)])
    level_mat, *row_mats = ordered(chunks, devices, one, vertical_cov, row_cov)

    def exchange(parts):
        got = [parts[0]] + [None] * (devices - 1)
        for span in (range(devices // 2, devices), range(devices // 2 - 1, 0, -1)):
            for s in span:
                got[s] = lax.ppermute(parts[s], "tile", [(t, t ^ s) for t in range(devices)])
        return got

    own = [mids, inner, far, near]
    ev = steps([2 * HALO], middle, one, inside, half_wind, kappa, own)
    mixed = mix_levels(devices, one, ev, [follow_mids], level_mat)
    first = exchange(mixed)

    *own, _ = lax.optimization_barrier((mids, inner, far, near, mixed[0]))
    follow_inner = earlier(own[1])
    follow_far, follow_near = earlier(own[2]), earlier(own[3])
    ev = steps([HALO, rows - 2 * HALO], HALO, one, inside, half_wind, kappa, own)
    mixed = mix_levels(devices, one, ev, [follow_inner], level_mat)
    second = exchange(mixed)

    *own, _ = lax.optimization_barrier((*own, mixed[0]))
    ev = steps([0, rows - HALO], HALO, one, inside, half_wind, kappa, own, [far_in, near_in])
    halves = levels // devices // SUB
    mixed = mix_levels(devices * halves, one, ev, [follow_far, follow_near], level_mat, column_cov)
    base = mix_rows(column_cov, row_mats[:2], [first, second])
    out = None
    for h in range(halves):
        last = exchange(mixed[h::halves])
        out = finish(h, row_mats[2], base, last, out)
    return out[None]


def with_halo(cells, sides, width):
    for axis, dim in sides:
        count = lax.axis_size(axis)
        ends = count - 1
        head = lax.slice_in_dim(cells, 0, width, axis=dim)
        tail = lax.slice_in_dim(cells, cells.shape[dim] - width, cells.shape[dim], axis=dim)
        cells = jnp.concatenate(
            [
                lax.ppermute(tail, axis, [(i, (i + 1) % count) for i in range(ends)]),
                cells,
                lax.ppermute(head, axis, [((i + 1) % count, i) for i in range(ends)]),
            ],
            axis=dim,
        )
    return cells


def tendency(center, north, south, kappa, wind_col):
    east = jnp.roll(center, -1, axis=2)
    west = jnp.roll(center, 1, axis=2)
    stacked = jnp.pad(center, ((1, 1), (0, 0), (0, 0)))
    horiz = north + south + east + west - 4.0 * center
    vert = stacked[2:] + stacked[:-2] - 2.0 * center
    return center + kappa[None] * horiz + VMIX * vert + wind_col * (0.5 * (south - north))


def plain_body(increment, diffusivity, wind, vertical_cov, row_cov, column_cov):
    field, kappa, wind_col = increment[0], diffusivity[0], wind[0][:, None, None]
    current = field
    for _ in range(STEPS):
        padded = with_halo(current, (("tile", 1),), 1)
        current = tendency(current, padded[:, 2:], padded[:, :-2], kappa, wind_col)
    size = lax.axis_size("win")
    defect = current - lax.ppermute(field, "win", [(i + 1, i) for i in range(size - 1)])
    levels, rows, width = defect.shape
    high = lax.Precision.HIGHEST
    mixed = jnp.dot(vertical_cov.astype(F32), defect.reshape(levels, rows * width), precision=high)
    mixed = jnp.dot(mixed.reshape(levels * rows, width), column_cov.astype(F32), precision=high)
    mixed = lax.all_to_all(mixed.reshape(levels, rows, width), "tile", split_axis=0, concat_axis=1, tiled=True)
    return jnp.einsum("yk,zkx->zyx", row_cov.astype(F32), mixed, precision=high)[None]


def body(*args):
    levels, rows, width = args[0].shape[1:]
    devices = lax.axis_size("tile")
    own = levels // devices
    fits = (
        rows > 4 * HALO
        and rows % SUB == 0
        and levels % (2 * SUB) == 0
        and levels % devices == 0
        and own % SUB == 0
        and width % LANES == 0
        and devices & (devices - 1) == 0
        and devices % SUB == 0
    )
    return tiled_body(*args) if fits else plain_body(*args)


def solution(mesh):
    in_specs = (P("win", None, "tile", None), P("win", "tile", None), P("win", None), P(), P(), P())
    out_specs = P("win", "tile", None, None)
    return jax.shard_map(body, mesh=mesh, in_specs=in_specs, out_specs=out_specs, check_vma=False)
```

```python
import functools

import jax
import jax.numpy as jnp
from jax import lax
from jax.experimental import pallas as pl
from jax.experimental.pallas import tpu as pltpu
from jax.sharding import PartitionSpec as P


STEPS = 6
VMIX = 0.1
SUB = 8
HALO = STEPS
LANES = 128
FIRST = 4
RELAY = False


F32 = jnp.float32
BF16 = jnp.bfloat16
ANY = pl.BlockSpec(memory_space=pl.ANY)
VM = pl.BlockSpec(memory_space=pltpu.VMEM)
SM = pl.BlockSpec(memory_space=pltpu.SMEM)


def params(limit_mib, sem=None):
    return pltpu.CompilerParams(vmem_limit_bytes=limit_mib << 20, dimension_semantics=sem)


def cost(flops, moved):
    return pl.CostEstimate(flops=int(flops), transcendentals=0, bytes_accessed=int(moved))


def iota(shape, dim):
    return lax.broadcasted_iota(jnp.int32, shape, dim)


def split(x):
    hi = x.astype(BF16)
    lo = (x - hi.astype(F32)).astype(BF16)
    return hi, lo


def mm(a, b):
    return jnp.dot(a, b, preferred_element_type=F32)


def one_hot(match):
    return match.astype(F32).astype(BF16)


def turn(parts):
    parts = list(parts)
    sub = iota(parts[0].shape, 0)
    for d in (4, 2, 1):
        low = (sub & d) == 0
        for i in range(SUB):
            if i & d == 0:
                a, b = parts[i], parts[i + d]
                parts[i] = jnp.where(low, a, pltpu.roll(b, d, axis=0))
                parts[i + d] = jnp.where(low, pltpu.roll(a, SUB - d, axis=0), b)
    return parts


def column_order(width):
    tiles = width // LANES
    at = iota((width, width), 1)
    return one_hot(iota((width, width), 0) == (at & (LANES - 1)) * tiles + (at >> (LANES.bit_length() - 1)))


def reorder(x, order):
    hi, lo = split(x)
    return mm(hi, order) + mm(lo, order)


def edge_rows(source, is_top):
    flat = turn(source)
    return flat[:HALO] if is_top else flat[SUB - HALO :]


def far_kernel(me_ref, top_ref, bottom_ref, kap_ref, far_ref, order):
    _, per, _, width = top_ref.shape
    rows = kap_ref.shape[0]
    blocks = per * pl.num_programs(0)
    step = pl.program_id(0)
    even = (me_ref[0] & 1) == 0

    @pl.when(step == 0)
    def _():
        order[...] = column_order(width)
        kapx = reorder(kap_ref[...], order[...])
        far_ref[HALO * blocks] = jnp.where(even, kapx[:SUB, :], kapx[rows - SUB :, :])

    for is_top, source in ((True, top_ref), (False, bottom_ref)):

        @pl.when(even == is_top)
        def _(is_top=is_top, source=source):
            flat = []
            for p in range(per):
                flat += edge_rows([source[s, p] for s in range(SUB)], is_top)
            moved = reorder(jnp.concatenate(flat, axis=0), order[...])
            for p in range(per):
                for row in range(HALO):
                    at = (p * HALO + row) * SUB
                    far_ref[row * blocks + step * per + p] = moved[at : at + SUB]


def far_edge(raw, kappa, me):
    levels, rows, width = raw.shape
    blocks = levels // SUB
    per = 4 if blocks % 4 == 0 else 2
    count = HALO * blocks + 1
    parts = raw.reshape(SUB, blocks, rows, width)
    last = rows // SUB - 1
    return pl.pallas_call(
        far_kernel,
        name="far_edge",
        grid=(blocks // per,),
        in_specs=[
            SM,
            pl.BlockSpec((SUB, per, SUB, width), lambda i: (0, i, 0, 0)),
            pl.BlockSpec((SUB, per, SUB, width), lambda i: (0, i, last, 0)),
            pl.BlockSpec((rows, width), lambda i: (0, 0)),
        ],
        out_specs=pl.BlockSpec((count, SUB, width), lambda i: (0, 0, 0)),
        out_shape=jax.ShapeDtypeStruct((count, SUB, width), F32),
        scratch_shapes=[pltpu.VMEM((width, width), BF16)],
        compiler_params=params(60),
        cost_estimate=cost(0, 3 * raw.size),
    )(me, parts, parts, kappa)


def pieces_kernel(cuts, me_ref, raw_ref, kap_ref, *rest):
    refs, near_ref, kapx_ref, order = rest[:-3], rest[-3], rest[-2], rest[-1]
    _, per, rows, width = raw_ref.shape
    step = pl.program_id(0)
    blocks = per * pl.num_programs(0)
    even = (me_ref[0] & 1) == 0

    @pl.when(step == 0)
    def _():
        order[...] = column_order(width)
        kapx = reorder(kap_ref[...], order[...])
        kapx_ref[...] = kapx
        near_ref[HALO * blocks] = jnp.where(even, kapx[rows - SUB :, :], kapx[:SUB, :])

    for p in range(per):
        flat = []
        for tile in range(rows // SUB):
            flat += turn([raw_ref[s, p, tile * SUB : (tile + 1) * SUB, :] for s in range(SUB)])
        edge = [jnp.where(even, b, a) for a, b in zip(flat[:HALO], flat[rows - HALO :])]
        moved = reorder(jnp.concatenate(flat[HALO : rows - HALO] + edge, axis=0), order[...])
        for (first, count), ref in zip(cuts, refs):
            for i in range(count):
                at = (first - HALO + i) * SUB
                ref[i, p] = moved[at : at + SUB]
        for i in range(HALO):
            at = (rows - 2 * HALO + i) * SUB
            near_ref[i * blocks + step * per + p] = moved[at : at + SUB]


def pieces(raw, kappa, cuts, me):
    levels, rows, width = raw.shape
    blocks = levels // SUB
    per = 2
    near = (HALO * blocks + 1, SUB, width)
    *parts, near, kapx = pl.pallas_call(
        functools.partial(pieces_kernel, cuts),
        name="pieces",
        grid=(blocks // per,),
        in_specs=[
            SM,
            pl.BlockSpec((SUB, per, rows, width), lambda i: (0, i, 0, 0)),
            pl.BlockSpec((rows, width), lambda i: (0, 0)),
        ],
        out_specs=[pl.BlockSpec((n, per, SUB, width), lambda i: (0, i, 0, 0)) for _, n in cuts]
        + [pl.BlockSpec(near, lambda i: (0, 0, 0)), pl.BlockSpec((rows, width), lambda i: (0, 0))],
        out_shape=[jax.ShapeDtypeStruct((n, blocks, SUB, width), F32) for _, n in cuts]
        + [jax.ShapeDtypeStruct(near, F32), jax.ShapeDtypeStruct((rows, width), F32)],
        scratch_shapes=[pltpu.VMEM((width, width), BF16)],
        compiler_params=params(60),
        cost_estimate=cost(4 * raw.size * width, 8 * raw.size),
    )(me, raw.reshape(SUB, blocks, rows, width), kappa)
    return *[x.reshape(x.shape[0] * blocks, SUB, width) for x in parts], near, kapx


def steps_kernel(plans, firsts, halos, me_ref, inside_ref, hw_ref, kap_ref, *rest):
    extra = 1 if halos else 0
    sources = rest[: len(rest) - 6 - 2 * extra]
    out_ref, ping, pong, kap, keep, sems = rest[len(sources) : len(sources) + 6]
    window, _, _, width = ping.shape
    blocks = ping.shape[1] - 2
    own = window - HALO
    seg = pl.program_id(0)
    even = (me_ref[0] & 1) == 0

    def copies(plan):
        return [
            pltpu.make_async_copy(
                sources[k].at[pl.ds(row * blocks, blocks)], ping.at[to, pl.ds(1, blocks)], sems.at[to]
            )
            for k, row, to in plan
        ]

    def edge_copy(k):
        return pltpu.make_async_copy(sources[k].at[HALO * blocks], rest[-2], rest[-1])

    for (g, parity), (plan, halo) in plans.items():
        here = seg == g if parity is None else (seg == g) & (even == (parity == 0))

        @pl.when(here)
        def _(plan=plan, halo=halo):
            for c in copies(plan):
                c.start()
            if halos:
                edge_copy(halo).start()
                edge_copy(halo).wait()

    def set_rows(r, row):
        row = jnp.broadcast_to(row, (SUB, width))
        kap[r] = row
        keep[r] = (1.0 - 2.0 * VMIX) - 4.0 * row

    first = firsts[0] if len(firsts) == 1 else jnp.where(seg == 0, firsts[0], firsts[1])
    if halos:
        at = jnp.where(seg == 0, HALO, 0)
        for r in range(own):
            set_rows(at + r, kap_ref[pl.ds(first + at + r, 1), :])
        edge_at, skip = jnp.where(seg == 0, 0, own), jnp.where(seg == 0, SUB - HALO, 0)
        for r in range(HALO):
            set_rows(edge_at + r, rest[-2][pl.ds(skip + r, 1), :])
    else:
        for r in range(window):
            set_rows(r, kap_ref[pl.ds(first + r, 1), :])
    sub = iota((SUB, width), 0)
    for (g, parity), (plan, _) in plans.items():
        here = seg == g if parity is None else (seg == g) & (even == (parity == 0))

        @pl.when(here)
        def _(plan=plan):
            for c in copies(plan):
                c.wait()

    def ghosts(ref, r, first_block, last_block):
        ref[r, 0] = jnp.where(sub == 0, 0.0, pltpu.roll(last_block, 1, axis=0))
        ref[r, blocks + 1] = jnp.where(sub == SUB - 1, 0.0, pltpu.roll(first_block, SUB - 1, axis=0))

    def ready(r, _):
        ghosts(ping, r, ping[r, 1], ping[r, blocks])
        return 0

    lax.fori_loop(0, window, ready, 0)

    tiles = width // LANES

    def advance(src, dst, r, factor, final):
        def load(row, i):
            return [src[row, i, :, k * LANES : (k + 1) * LANES] for k in range(tiles)]

        before, center = load(r, 0), load(r, 1)
        head = tail = None
        for i in range(1, blocks + 1):
            after, up, down = load(r, i + 1), load(r + 1, i), load(r - 1, i)
            wind = hw_ref[i - 1]
            line = [pltpu.roll(center[-1], 1, axis=1), *center, pltpu.roll(center[0], LANES - 1, axis=1)]
            new = []
            for k in range(tiles):
                west, east = line[k], line[k + 2]
                cols = slice(k * LANES, (k + 1) * LANES)
                value = (
                    keep[r, :, cols] * center[k]
                    + kap[r, :, cols] * ((east + west) + (up[k] + down[k]))
                    + (VMIX * (before[k] + after[k]) + wind * (down[k] - up[k]))
                )
                new.append(value if factor is None else value * factor)
            for k in range(tiles):
                cols = slice(k * LANES, (k + 1) * LANES)
                if final:
                    out_ref[r - HALO, i - 1, :, cols] = new[k]
                else:
                    dst[r, i, :, cols] = new[k]
            head = jnp.concatenate(new, axis=1) if i == 1 else head
            if i == blocks:
                tail = jnp.concatenate(new, axis=1)
            before, center = center, after
        if not final:
            ghosts(dst, r, head, tail)

    refs = (ping, pong)
    for step in range(STEPS):
        src, dst = refs[step % 2], refs[(step + 1) % 2]
        final = step == STEPS - 1
        low, high = step + 1, window - 1 - step

        def body(r, _, src=src, dst=dst, final=final):
            advance(src, dst, r, None, final)
            return 0

        if halos and not final:
            inside = inside_ref[seg]

            def masked(r, _, src=src, dst=dst):
                advance(src, dst, r, inside, False)
                return 0

            up_side = seg == 0
            lax.fori_loop(jnp.where(up_side, low, own), jnp.where(up_side, HALO, high), masked, 0)
            lax.fori_loop(jnp.where(up_side, HALO, low), jnp.where(up_side, high, own), body, 0)
        else:
            lax.fori_loop(low, high, body, 0)


def steps(firsts, count, me, inside, half_wind, kappa, cuts, sources, halo_sources=None, limit=24):
    rows, width = kappa.shape
    blocks = half_wind.shape[0]
    window = count + 2 * HALO
    halos = halo_sources is not None
    arrays = [*sources, *(halo_sources or [])]

    def locate(row, parity):
        far, near = len(cuts), len(cuts) + 1
        first, second = (far, near) if parity == 0 else (near, far)
        if row < 0:
            return first + 2, row + HALO
        if row >= rows:
            return second + 2, row - rows
        if row < HALO:
            return first, row
        if row >= rows - HALO:
            return second, row - rows + HALO
        return next((k, row - start) for k, (start, n) in enumerate(cuts) if start <= row < start + n)

    plans = {}
    for g, f in enumerate(firsts):
        for parity in (0, 1):
            plan = [(*locate(f - HALO + r, parity), r) for r in range(window)]
            plans[g, parity] = (plan, len(cuts) + (2 if (g == 0) == (parity == 0) else 3))
    used = sorted({k for plan, _ in plans.values() for k, _, _ in plan})
    plans = {
        key: ([(used.index(k), row, to) for k, row, to in plan], used.index(halo) if halos else None)
        for key, (plan, halo) in plans.items()
    }
    n = len(firsts)
    updates = n * sum(window - 2 - 2 * s for s in range(STEPS)) * blocks * SUB * width
    extra = [pltpu.VMEM((SUB, width), F32), pltpu.SemaphoreType.DMA] if halos else []
    return pl.pallas_call(
        functools.partial(steps_kernel, plans, [f - HALO for f in firsts], halos),
        grid=(n,),
        in_specs=[SM, SM, VM, VM] + [ANY] * len(used),
        out_specs=pl.BlockSpec((count, blocks, SUB, width), lambda i: (i, 0, 0, 0)),
        out_shape=jax.ShapeDtypeStruct((n * count, blocks, SUB, width), F32),
        scratch_shapes=[
            pltpu.VMEM((window, blocks + 2, SUB, width), F32),
            pltpu.VMEM((window, blocks + 2, SUB, width), F32),
            pltpu.VMEM((window, SUB, width), F32),
            pltpu.VMEM((window, SUB, width), F32),
            pltpu.SemaphoreType.DMA((window,)),
            *extra,
        ],
        compiler_params=params(limit),
        cost_estimate=cost(14 * updates, 4 * n * (window + count) * blocks * SUB * width),
    )(me, inside, half_wind, kappa, *[arrays[k] for k in used])


def order_levels_kernel(devices, me_ref, vert_ref, out_ref):
    levels = vert_ref.shape[0]
    own, blocks = levels // devices, levels // SUB
    at = iota((levels, levels), 0)
    partner = sum((at >= s * own).astype(jnp.int32) for s in range(1, devices))
    left = one_hot(iota((levels, levels), 1) == (partner ^ me_ref[0]) * own + (at - partner * own))
    at = iota((levels, levels), 1)
    block, sub = at >> (SUB.bit_length() - 1), at & (SUB - 1)
    right = one_hot(iota((levels, levels), 0) == sub * blocks + block)
    out_ref[...] = mm(mm(left, vert_ref[...]).astype(BF16), right).astype(BF16)


def order_levels(devices, me, vert):
    return pl.pallas_call(
        functools.partial(order_levels_kernel, devices),
        name="order_levels",
        in_specs=[SM, VM],
        out_specs=VM,
        out_shape=jax.ShapeDtypeStruct(vert.shape, BF16),
        compiler_params=params(8),
        cost_estimate=cost(4 * vert.size * vert.shape[0], 4 * vert.size),
    )(me, vert)


def order_rest_kernel(chunks, devices, me_ref, row_ref, col_ref, colx_ref, *outs):
    rows = row_ref.shape[0]
    here = rows // devices
    flip = (((0,), (0,)), ((), ()))
    pick = column_order(col_ref.shape[0])
    colx_ref[...] = lax.dot_general(pick, col_ref[...], flip, preferred_element_type=F32).astype(BF16)
    for segments, ref in zip(chunks, outs):
        count = sum(n for _, n in segments)
        at = iota((rows, 2 * count * devices), 1)
        at = jnp.where(at >= count * devices, at - count * devices, at)
        partner = sum((at >= s * count).astype(jnp.int32) for s in range(1, devices))
        within = at - partner * count
        source = within + segments[0][0]
        base = 0
        for (first, n), (after, _) in zip(segments, segments[1:]):
            base += n
            source = source + jnp.where(within >= base, after - first - n, 0)
        pick = one_hot(iota((rows, 2 * count * devices), 0) == (partner ^ me_ref[0]) * here + source)
        ref[...] = mm(row_ref[...], pick).astype(BF16)


def order_rest(chunks, devices, me, row, col):
    rows = row.shape[0]
    widths = [2 * devices * sum(n for _, n in segments) for segments in chunks]
    return pl.pallas_call(
        functools.partial(order_rest_kernel, chunks, devices),
        name="order_rest",
        in_specs=[SM, VM, VM],
        out_specs=[VM] * (1 + len(chunks)),
        out_shape=[jax.ShapeDtypeStruct(col.shape, BF16)]
        + [jax.ShapeDtypeStruct((rows, w), BF16) for w in widths],
        compiler_params=params(16),
        cost_estimate=cost(2 * rows * rows * rows, 4 * rows * rows),
    )(me, row, col)


def levels_kernel(edges, with_columns, me_ref, ev_ref, mat_ref, *rest):
    fo_refs, rest = rest[: 2 if edges else 1], rest[2 if edges else 1 :]
    col_ref, outs = (rest[0], rest[1:]) if with_columns else (None, rest)
    per, blocks, sub, width = ev_ref.shape
    own = outs[0].shape[1]
    late = (pl.program_id(0) >= pl.num_programs(0) // 2).astype(jnp.int32)
    near = late != (me_ref[0] & 1)
    mat = mat_ref[...]
    for r in range(per):
        following = fo_refs[0][r * blocks : (r + 1) * blocks]
        if edges:
            following = jnp.where(near, fo_refs[1][r * blocks : (r + 1) * blocks], following)
        hi, lo = split((ev_ref[r] - following).reshape(blocks * sub, width))
        mixed = mm(mat, hi) + mm(mat, lo)
        if with_columns:
            hi, lo = split(mixed)
            mixed = mm(hi, col_ref[...]) + mm(lo, col_ref[...])
        for s, ref in enumerate(outs):
            ref[r] = mixed[s * own : (s + 1) * own]


def mix_levels(count, me, evolved, following, mat, col=None):
    rows, blocks, sub, width = evolved.shape
    levels = blocks * sub
    own = levels // count
    per = 2
    edges = len(following) == 2
    half = rows // (2 * per)
    spec = pl.BlockSpec((per * blocks, sub, width), lambda i: (lax.rem(i, half) if edges else i, 0, 0))
    cols = [] if col is None else [col]
    return pl.pallas_call(
        functools.partial(levels_kernel, edges, col is not None),
        name="mix_levels",
        grid=(rows // per,),
        in_specs=[
            SM,
            pl.BlockSpec((per, blocks, sub, width), lambda i: (i, 0, 0, 0)),
            pl.BlockSpec(mat.shape, lambda i: (0, 0)),
        ]
        + [spec] * len(following)
        + [pl.BlockSpec(c.shape, lambda i: (0, 0)) for c in cols],
        out_specs=[pl.BlockSpec((per, own, width), lambda i: (i, 0, 0))] * count,
        out_shape=[jax.ShapeDtypeStruct((rows, own, width), F32)] * count,
        compiler_params=params(16),
        cost_estimate=cost(4 * levels * levels * rows * width, 12 * evolved.size),
    )(me, evolved, mat, *following, *cols)


def by_level(x):
    groups = [turn([x[g + i] for i in range(SUB)]) for g in range(0, x.shape[0], SUB)]
    return [jnp.concatenate([g[z] for g in groups], axis=0) for z in range(SUB)]


def stacked(x):
    return jnp.concatenate(split(x), axis=0)


def rows_kernel(counts, added, col_ref, *rest):
    mats, xs, out_ref = rest[: len(counts)], rest[len(counts) : -1], rest[-1]
    extra = dict(zip(added, xs[sum(counts) :]))
    width = out_ref.shape[2]
    totals = [None] * SUB
    start = 0
    for mat_ref, count in zip(mats, counts):
        parts = [xs[i][...] + extra[i][...] if i in extra else xs[i][...] for i in range(start, start + count)]
        x = jnp.concatenate(parts, axis=0)
        start += count
        depth = x.shape[0]
        hi, lo = split(x.reshape(depth * SUB, width))
        mixed = (mm(hi, col_ref[...]) + mm(lo, col_ref[...])).reshape(depth, SUB, width)
        for z, level in enumerate(by_level(mixed)):
            part = mm(mat_ref[...], stacked(level))
            totals[z] = part if totals[z] is None else totals[z] + part
    for z in range(SUB):
        out_ref[z] = totals[z]


def mix_rows(col, mats, groups, moved):
    blocks = [x for group in groups for x in group]
    own, width = blocks[0].shape[1:]
    rows = mats[0].shape[0]
    depth = sum(x.shape[0] for x in blocks)
    return pl.pallas_call(
        functools.partial(rows_kernel, [len(g) for g in groups], list(moved)),
        name="mix_rows",
        grid=(own // SUB,),
        in_specs=[pl.BlockSpec(m.shape, lambda i: (0, 0)) for m in [col, *mats]]
        + [pl.BlockSpec((x.shape[0], SUB, width), lambda i: (0, i, 0)) for x in [*blocks, *moved.values()]],
        out_specs=pl.BlockSpec((SUB, rows, width), lambda i: (i, 0, 0)),
        out_shape=jax.ShapeDtypeStruct((own, rows, width), F32),
        compiler_params=params(36),
        cost_estimate=cost(4 * own * depth * width * (width + rows), 4 * own * width * (depth + rows)),
    )(col, *mats, *blocks, *moved.values())


def finish_kernel(count, mat_ref, base_ref, *rest):
    out_ref = rest[-1]
    x = jnp.concatenate([ref[...] for ref in rest[:count]], axis=0)
    for z, level in enumerate(by_level(x)):
        out_ref[z] = base_ref[z] + mm(mat_ref[...], stacked(level))


def finish(part, mat, base, blocks, out=None):
    _, rows, width = base.shape
    cols = 2 * LANES if width % (2 * LANES) == 0 else LANES
    spec = pl.BlockSpec((SUB, rows, cols), lambda j: (part, 0, j))
    rest = [] if out is None else [out]
    depth = sum(x.shape[0] for x in blocks)
    return pl.pallas_call(
        functools.partial(finish_kernel, len(blocks)),
        name="finish",
        grid=(width // cols,),
        in_specs=[pl.BlockSpec(mat.shape, lambda j: (0, 0)), spec]
        + [pl.BlockSpec((x.shape[0], SUB, cols), lambda j: (0, 0, j)) for x in blocks]
        + [ANY] * len(rest),
        out_specs=spec,
        out_shape=jax.ShapeDtypeStruct(base.shape, F32),
        input_output_aliases={2 + len(blocks): 0} if rest else {},
        compiler_params=params(16),
        cost_estimate=cost(4 * SUB * depth * rows * width, 4 * SUB * width * (depth + 2 * rows)),
    )(mat, base, *blocks, *rest)


def tiled_body(increment, diffusivity, wind, vertical_cov, row_cov, column_cov):
    raw, kappa = increment[0], diffusivity[0]
    devices, windows = lax.axis_size("tile"), lax.axis_size("win")
    levels, rows, _ = raw.shape
    blocks = levels // SUB
    me = lax.axis_index("tile").astype(jnp.int32)
    half_wind = jnp.broadcast_to((0.5 * wind[0]).reshape(SUB, blocks).T[:, :, None], (blocks, SUB, LANES))
    inside = jnp.stack([me != 0, me != devices - 1]).astype(F32)
    half = rows // 2
    side = half - FIRST // 2 - HALO
    cuts = ((half - FIRST // 2, FIRST), (HALO, side), (half + FIRST // 2, side))
    chunks = tuple((c,) for c in cuts) + (((0, HALO), (rows - HALO, HALO)),)
    one = me.reshape(1)
    far = far_edge(raw, kappa, one)
    *parts, near, kappa = pieces(raw, kappa, cuts, one)

    def earlier(x):
        return lax.ppermute(x, "win", [(i + 1, i) for i in range(windows - 1)])

    apart = [(t, t + 1) for t in range(1, devices - 1, 2)] + [(t + 1, t) for t in range(1, devices - 1, 2)]
    far_in = lax.ppermute(far, "tile", apart)
    follow = [earlier(parts[0])]
    follow.append(earlier(parts[1]))
    near_in = lax.ppermute(near, "tile", [(t, t ^ 1) for t in range(devices)])
    level_mat = order_levels(devices, one, vertical_cov)

    def exchange(mixed, without={}):
        got = [mixed[0]] + [None] * (devices - 1)
        for span in (range(devices // 2, devices), range(devices // 2 - 1, 0, -1)):
            for s in span:
                pairs = [(t, t ^ s) for t in range(devices) if t not in without.get(s, ())]
                got[s] = lax.ppermute(mixed[s], "tile", pairs)
        return got

    cross = devices // 2 + 1
    movers = [devices // 2 - 1, devices // 2] if devices == 8 and RELAY else []
    groups = []
    own = [*parts, far, near]
    for j, (first, count) in enumerate(cuts):
        ev = steps([first], count, one, inside, half_wind, kappa, cuts, own)
        mixed = mix_levels(devices, one, ev, [follow[j]], level_mat)
        groups.append(exchange(mixed, {cross: movers} if j == 1 else {}))
        if j == 1 and movers:
            aside = lax.ppermute(mixed[cross], "tile", [(t, t ^ 1) for t in movers])
        *own, _ = lax.optimization_barrier((*own, mixed[0]))
        if j == 0:
            follow.append(earlier(own[2]))
        elif j == 1:
            row, col, _ = lax.optimization_barrier((row_cov, column_cov, mixed[0]))
            col_mat, *row_mats = order_rest(chunks, devices, one, row, col)
            follow_edges = [earlier(own[3]), earlier(own[4])]
    moved = {}
    if movers:
        aside = lax.ppermute(aside, "tile", [(t ^ 1, t ^ cross) for t in movers])
        moved = {devices + cross: aside}

    ev = steps([0, rows - HALO], HALO, one, inside, half_wind, kappa, cuts, own, [far_in, near_in])
    halves = levels // devices // SUB
    mixed = mix_levels(devices * halves, one, ev, follow_edges, level_mat, col_mat)
    base = mix_rows(col_mat, row_mats[:3], groups, moved)
    out = None
    for h in range(halves):
        last = exchange(mixed[h::halves])
        out = finish(h, row_mats[3], base, last, out)
    return out[None]


def with_halo(cells, sides, width):
    for axis, dim in sides:
        count = lax.axis_size(axis)
        ends = count - 1
        head = lax.slice_in_dim(cells, 0, width, axis=dim)
        tail = lax.slice_in_dim(cells, cells.shape[dim] - width, cells.shape[dim], axis=dim)
        cells = jnp.concatenate(
            [
                lax.ppermute(tail, axis, [(i, (i + 1) % count) for i in range(ends)]),
                cells,
                lax.ppermute(head, axis, [((i + 1) % count, i) for i in range(ends)]),
            ],
            axis=dim,
        )
    return cells


def tendency(center, north, south, kappa, wind_col):
    east = jnp.roll(center, -1, axis=2)
    west = jnp.roll(center, 1, axis=2)
    stacked = jnp.pad(center, ((1, 1), (0, 0), (0, 0)))
    horiz = north + south + east + west - 4.0 * center
    vert = stacked[2:] + stacked[:-2] - 2.0 * center
    return center + kappa[None] * horiz + VMIX * vert + wind_col * (0.5 * (south - north))


def plain_body(increment, diffusivity, wind, vertical_cov, row_cov, column_cov):
    field, kappa, wind_col = increment[0], diffusivity[0], wind[0][:, None, None]
    current = field
    for _ in range(STEPS):
        padded = with_halo(current, (("tile", 1),), 1)
        current = tendency(current, padded[:, 2:], padded[:, :-2], kappa, wind_col)
    size = lax.axis_size("win")
    defect = current - lax.ppermute(field, "win", [(i + 1, i) for i in range(size - 1)])
    levels, rows, width = defect.shape
    high = lax.Precision.HIGHEST
    mixed = jnp.dot(vertical_cov.astype(F32), defect.reshape(levels, rows * width), precision=high)
    mixed = jnp.dot(mixed.reshape(levels * rows, width), column_cov.astype(F32), precision=high)
    mixed = lax.all_to_all(mixed.reshape(levels, rows, width), "tile", split_axis=0, concat_axis=1, tiled=True)
    return jnp.einsum("yk,zkx->zyx", row_cov.astype(F32), mixed, precision=high)[None]


def body(*args):
    levels, rows, width = args[0].shape[1:]
    devices = lax.axis_size("tile")
    own = levels // devices
    fits = (
        rows >= 2 * HALO + 2 * SUB + FIRST
        and rows % SUB == 0
        and levels % (2 * SUB) == 0
        and levels % devices == 0
        and own % SUB == 0
        and width % LANES == 0
        and devices & (devices - 1) == 0
        and devices % SUB == 0
    )
    return tiled_body(*args) if fits else plain_body(*args)


def solution(mesh):
    in_specs = (P("win", None, "tile", None), P("win", "tile", None), P("win", None), P(), P(), P())
    out_specs = P("win", "tile", None, None)


    return jax.shard_map(body, mesh=mesh, in_specs=in_specs, out_specs=out_specs, check_vma=False)
```

```python
import functools

import jax
import jax.numpy as jnp
from jax import lax
from jax.experimental import pallas as pl
from jax.experimental.pallas import tpu as pltpu
from jax.sharding import PartitionSpec as P


STEPS = 6
VMIX = 0.1
SUB = 8
HALO = STEPS
LANES = 128
FIRST = 4


F32 = jnp.float32
BF16 = jnp.bfloat16
ANY = pl.BlockSpec(memory_space=pl.ANY)
VM = pl.BlockSpec(memory_space=pltpu.VMEM)
SM = pl.BlockSpec(memory_space=pltpu.SMEM)


def params(limit_mib, sem=None):
    return pltpu.CompilerParams(vmem_limit_bytes=limit_mib << 20, dimension_semantics=sem)


def cost(flops, moved):
    return pl.CostEstimate(flops=int(flops), transcendentals=0, bytes_accessed=int(moved))


def iota(shape, dim):
    return lax.broadcasted_iota(jnp.int32, shape, dim)


def split(x):
    hi = x.astype(BF16)
    lo = (x - hi.astype(F32)).astype(BF16)
    return hi, lo


def mm(a, b):
    return jnp.dot(a, b, preferred_element_type=F32)


def one_hot(match):
    return match.astype(F32).astype(BF16)


def turn(parts):
    parts = list(parts)
    sub = iota(parts[0].shape, 0)
    for d in (4, 2, 1):
        low = (sub & d) == 0
        for i in range(SUB):
            if i & d == 0:
                a, b = parts[i], parts[i + d]
                parts[i] = jnp.where(low, a, pltpu.roll(b, d, axis=0))
                parts[i + d] = jnp.where(low, pltpu.roll(a, SUB - d, axis=0), b)
    return parts


def column_order(width):
    tiles = width // LANES
    at = iota((width, width), 1)
    return one_hot(iota((width, width), 0) == (at & (LANES - 1)) * tiles + (at >> (LANES.bit_length() - 1)))


def reorder(x, order):
    hi, lo = split(x)
    return mm(hi, order) + mm(lo, order)


def far_kernel(me_ref, tile_ref, kap_ref, far_ref, order):
    _, per, _, width = tile_ref.shape
    rows = kap_ref.shape[0]
    blocks = per * pl.num_programs(0)
    step = pl.program_id(0)
    even = (me_ref[0] & 1) == 0

    @pl.when(step == 0)
    def _():
        order[...] = column_order(width)
        kapx = reorder(kap_ref[...], order[...])
        far_ref[HALO * blocks] = jnp.where(even, kapx[:SUB, :], kapx[rows - SUB :, :])

    flat = []
    for p in range(per):
        turned = turn([tile_ref[s, p] for s in range(SUB)])
        flat += [jnp.where(even, turned[i], turned[i + SUB - HALO]) for i in range(HALO)]
    moved = reorder(jnp.concatenate(flat, axis=0), order[...])
    for p in range(per):
        for row in range(HALO):
            at = (p * HALO + row) * SUB
            far_ref[row * blocks + step * per + p] = moved[at : at + SUB]


def far_edge(raw, kappa, me):
    levels, rows, width = raw.shape
    blocks = levels // SUB
    per = 4 if blocks % 4 == 0 else 2
    count = HALO * blocks + 1
    parts = raw.reshape(SUB, blocks, rows, width)
    last = rows // SUB - 1
    return pl.pallas_call(
        far_kernel,
        name="far_edge",
        grid_spec=pltpu.PrefetchScalarGridSpec(
            num_scalar_prefetch=1,
            grid=(blocks // per,),
            in_specs=[
                pl.BlockSpec((SUB, per, SUB, width), lambda i, at: (0, i, (at[0] & 1) * last, 0)),
                pl.BlockSpec((rows, width), lambda i, at: (0, 0)),
            ],
            out_specs=pl.BlockSpec((count, SUB, width), lambda i, at: (0, 0, 0)),
            scratch_shapes=[pltpu.VMEM((width, width), BF16)],
        ),
        out_shape=jax.ShapeDtypeStruct((count, SUB, width), F32),
        compiler_params=params(60),
        cost_estimate=cost(0, 3 * raw.size),
    )(me, parts, kappa)


def pieces_kernel(cuts, me_ref, raw_ref, kap_ref, *rest):
    refs, near_ref, kapx_ref, order = rest[:-3], rest[-3], rest[-2], rest[-1]
    _, per, rows, width = raw_ref.shape
    step = pl.program_id(0)
    blocks = per * pl.num_programs(0)
    even = (me_ref[0] & 1) == 0

    @pl.when(step == 0)
    def _():
        order[...] = column_order(width)
        kapx = reorder(kap_ref[...], order[...])
        kapx_ref[...] = kapx
        near_ref[HALO * blocks] = jnp.where(even, kapx[rows - SUB :, :], kapx[:SUB, :])

    for p in range(per):
        flat = []
        for tile in range(rows // SUB):
            flat += turn([raw_ref[s, p, tile * SUB : (tile + 1) * SUB, :] for s in range(SUB)])
        edge = [jnp.where(even, b, a) for a, b in zip(flat[:HALO], flat[rows - HALO :])]
        moved = reorder(jnp.concatenate(flat[HALO : rows - HALO] + edge, axis=0), order[...])
        for (first, count), ref in zip(cuts, refs):
            for i in range(count):
                at = (first - HALO + i) * SUB
                ref[i, p] = moved[at : at + SUB]
        for i in range(HALO):
            at = (rows - 2 * HALO + i) * SUB
            near_ref[i * blocks + step * per + p] = moved[at : at + SUB]


def pieces(raw, kappa, cuts, me):
    levels, rows, width = raw.shape
    blocks = levels // SUB
    per = 2
    near = (HALO * blocks + 1, SUB, width)
    *parts, near, kapx = pl.pallas_call(
        functools.partial(pieces_kernel, cuts),
        name="pieces",
        grid=(blocks // per,),
        in_specs=[
            SM,
            pl.BlockSpec((SUB, per, rows, width), lambda i: (0, i, 0, 0)),
            pl.BlockSpec((rows, width), lambda i: (0, 0)),
        ],
        out_specs=[pl.BlockSpec((n, per, SUB, width), lambda i: (0, i, 0, 0)) for _, n in cuts]
        + [pl.BlockSpec(near, lambda i: (0, 0, 0)), pl.BlockSpec((rows, width), lambda i: (0, 0))],
        out_shape=[jax.ShapeDtypeStruct((n, blocks, SUB, width), F32) for _, n in cuts]
        + [jax.ShapeDtypeStruct(near, F32), jax.ShapeDtypeStruct((rows, width), F32)],
        scratch_shapes=[pltpu.VMEM((width, width), BF16)],
        compiler_params=params(60),
        cost_estimate=cost(4 * raw.size * width, 8 * raw.size),
    )(me, raw.reshape(SUB, blocks, rows, width), kappa)
    return *[x.reshape(x.shape[0] * blocks, SUB, width) for x in parts], near, kapx


def steps_kernel(plans, firsts, halos, me_ref, inside_ref, hw_ref, kap_ref, *rest):
    extra = 1 if halos else 0
    sources = rest[: len(rest) - 6 - 2 * extra]
    out_ref, ping, pong, kap, keep, sems = rest[len(sources) : len(sources) + 6]
    window, _, _, width = ping.shape
    blocks = ping.shape[1] - 2
    own = window - HALO
    seg = pl.program_id(0)
    even = (me_ref[0] & 1) == 0

    def copies(plan):
        return [
            pltpu.make_async_copy(
                sources[k].at[pl.ds(row * blocks, blocks)], ping.at[to, pl.ds(1, blocks)], sems.at[to]
            )
            for k, row, to in plan
        ]

    def edge_copy(k):
        return pltpu.make_async_copy(sources[k].at[HALO * blocks], rest[-2], rest[-1])

    for (g, parity), (plan, halo) in plans.items():
        here = seg == g if parity is None else (seg == g) & (even == (parity == 0))

        @pl.when(here)
        def _(plan=plan, halo=halo):
            for c in copies(plan):
                c.start()
            if halos:
                edge_copy(halo).start()
                edge_copy(halo).wait()

    def set_rows(r, row):
        row = jnp.broadcast_to(row, (SUB, width))
        kap[r] = row
        keep[r] = (1.0 - 2.0 * VMIX) - 4.0 * row

    first = firsts[0] if len(firsts) == 1 else jnp.where(seg == 0, firsts[0], firsts[1])
    if halos:
        at = jnp.where(seg == 0, HALO, 0)
        for r in range(own):
            set_rows(at + r, kap_ref[pl.ds(first + at + r, 1), :])
        edge_at, skip = jnp.where(seg == 0, 0, own), jnp.where(seg == 0, SUB - HALO, 0)
        for r in range(HALO):
            set_rows(edge_at + r, rest[-2][pl.ds(skip + r, 1), :])
    else:
        for r in range(window):
            set_rows(r, kap_ref[pl.ds(first + r, 1), :])
    sub = iota((SUB, width), 0)
    for (g, parity), (plan, _) in plans.items():
        here = seg == g if parity is None else (seg == g) & (even == (parity == 0))

        @pl.when(here)
        def _(plan=plan):
            for c in copies(plan):
                c.wait()

    def ghosts(ref, r, first_block, last_block):
        ref[r, 0] = jnp.where(sub == 0, 0.0, pltpu.roll(last_block, 1, axis=0))
        ref[r, blocks + 1] = jnp.where(sub == SUB - 1, 0.0, pltpu.roll(first_block, SUB - 1, axis=0))

    def ready(r, _):
        ghosts(ping, r, ping[r, 1], ping[r, blocks])
        return 0

    lax.fori_loop(0, window, ready, 0)

    tiles = width // LANES

    def advance(src, dst, r, factor, final):
        def load(row, i):
            return [src[row, i, :, k * LANES : (k + 1) * LANES] for k in range(tiles)]

        before, center = load(r, 0), load(r, 1)
        head = tail = None
        for i in range(1, blocks + 1):
            after, up, down = load(r, i + 1), load(r + 1, i), load(r - 1, i)
            wind = hw_ref[i - 1]
            line = [pltpu.roll(center[-1], 1, axis=1), *center, pltpu.roll(center[0], LANES - 1, axis=1)]
            new = []
            for k in range(tiles):
                west, east = line[k], line[k + 2]
                cols = slice(k * LANES, (k + 1) * LANES)
                value = (
                    keep[r, :, cols] * center[k]
                    + kap[r, :, cols] * ((east + west) + (up[k] + down[k]))
                    + (VMIX * (before[k] + after[k]) + wind * (down[k] - up[k]))
                )
                new.append(value if factor is None else value * factor)
            for k in range(tiles):
                cols = slice(k * LANES, (k + 1) * LANES)
                if final:
                    out_ref[r - HALO, i - 1, :, cols] = new[k]
                else:
                    dst[r, i, :, cols] = new[k]
            head = jnp.concatenate(new, axis=1) if i == 1 else head
            if i == blocks:
                tail = jnp.concatenate(new, axis=1)
            before, center = center, after
        if not final:
            ghosts(dst, r, head, tail)

    refs = (ping, pong)
    for step in range(STEPS):
        src, dst = refs[step % 2], refs[(step + 1) % 2]
        final = step == STEPS - 1
        low, high = step + 1, window - 1 - step

        def body(r, _, src=src, dst=dst, final=final):
            advance(src, dst, r, None, final)
            return 0

        if halos and not final:
            inside = inside_ref[seg]

            def masked(r, _, src=src, dst=dst):
                advance(src, dst, r, inside, False)
                return 0

            up_side = seg == 0
            lax.fori_loop(jnp.where(up_side, low, own), jnp.where(up_side, HALO, high), masked, 0)
            lax.fori_loop(jnp.where(up_side, HALO, low), jnp.where(up_side, high, own), body, 0)
        else:
            lax.fori_loop(low, high, body, 0)


def steps(firsts, count, me, inside, half_wind, kappa, cuts, sources, halo_sources=None, limit=24):
    rows, width = kappa.shape
    blocks = half_wind.shape[0]
    window = count + 2 * HALO
    halos = halo_sources is not None
    arrays = [*sources, *(halo_sources or [])]

    def locate(row, parity):
        far, near = len(cuts), len(cuts) + 1
        first, second = (far, near) if parity == 0 else (near, far)
        if row < 0:
            return first + 2, row + HALO
        if row >= rows:
            return second + 2, row - rows
        if row < HALO:
            return first, row
        if row >= rows - HALO:
            return second, row - rows + HALO
        return next((k, row - start) for k, (start, n) in enumerate(cuts) if start <= row < start + n)

    plans = {}
    for g, f in enumerate(firsts):
        for parity in (0, 1):
            plan = [(*locate(f - HALO + r, parity), r) for r in range(window)]
            plans[g, parity] = (plan, len(cuts) + (2 if (g == 0) == (parity == 0) else 3))
    used = sorted({k for plan, _ in plans.values() for k, _, _ in plan})
    plans = {
        key: ([(used.index(k), row, to) for k, row, to in plan], used.index(halo) if halos else None)
        for key, (plan, halo) in plans.items()
    }
    n = len(firsts)
    updates = n * sum(window - 2 - 2 * s for s in range(STEPS)) * blocks * SUB * width
    extra = [pltpu.VMEM((SUB, width), F32), pltpu.SemaphoreType.DMA] if halos else []
    return pl.pallas_call(
        functools.partial(steps_kernel, plans, [f - HALO for f in firsts], halos),
        grid=(n,),
        in_specs=[SM, SM, VM, VM] + [ANY] * len(used),
        out_specs=pl.BlockSpec((count, blocks, SUB, width), lambda i: (i, 0, 0, 0)),
        out_shape=jax.ShapeDtypeStruct((n * count, blocks, SUB, width), F32),
        scratch_shapes=[
            pltpu.VMEM((window, blocks + 2, SUB, width), F32),
            pltpu.VMEM((window, blocks + 2, SUB, width), F32),
            pltpu.VMEM((window, SUB, width), F32),
            pltpu.VMEM((window, SUB, width), F32),
            pltpu.SemaphoreType.DMA((window,)),
            *extra,
        ],
        compiler_params=params(limit),
        cost_estimate=cost(14 * updates, 4 * n * (window + count) * blocks * SUB * width),
    )(me, inside, half_wind, kappa, *[arrays[k] for k in used])


def order_levels_kernel(devices, me_ref, vert_ref, out_ref):
    levels = vert_ref.shape[0]
    own, blocks = levels // devices, levels // SUB
    at = iota((levels, levels), 0)
    partner = sum((at >= s * own).astype(jnp.int32) for s in range(1, devices))
    left = one_hot(iota((levels, levels), 1) == (partner ^ me_ref[0]) * own + (at - partner * own))
    at = iota((levels, levels), 1)
    block, sub = at >> (SUB.bit_length() - 1), at & (SUB - 1)
    right = one_hot(iota((levels, levels), 0) == sub * blocks + block)
    out_ref[...] = mm(mm(left, vert_ref[...]).astype(BF16), right).astype(BF16)


def order_levels(devices, me, vert):
    return pl.pallas_call(
        functools.partial(order_levels_kernel, devices),
        name="order_levels",
        in_specs=[SM, VM],
        out_specs=VM,
        out_shape=jax.ShapeDtypeStruct(vert.shape, BF16),
        compiler_params=params(8),
        cost_estimate=cost(4 * vert.size * vert.shape[0], 4 * vert.size),
    )(me, vert)


def order_rest_kernel(chunks, devices, me_ref, row_ref, col_ref, colx_ref, *outs):
    rows = row_ref.shape[0]
    here = rows // devices
    flip = (((0,), (0,)), ((), ()))
    pick = column_order(col_ref.shape[0])
    colx_ref[...] = lax.dot_general(pick, col_ref[...], flip, preferred_element_type=F32).astype(BF16)
    for segments, ref in zip(chunks, outs):
        count = sum(n for _, n in segments)
        at = iota((rows, 2 * count * devices), 1)
        at = jnp.where(at >= count * devices, at - count * devices, at)
        partner = sum((at >= s * count).astype(jnp.int32) for s in range(1, devices))
        within = at - partner * count
        source = within + segments[0][0]
        base = 0
        for (first, n), (after, _) in zip(segments, segments[1:]):
            base += n
            source = source + jnp.where(within >= base, after - first - n, 0)
        pick = one_hot(iota((rows, 2 * count * devices), 0) == (partner ^ me_ref[0]) * here + source)
        ref[...] = mm(row_ref[...], pick).astype(BF16)


def order_rest(chunks, devices, me, row, col):
    rows = row.shape[0]
    widths = [2 * devices * sum(n for _, n in segments) for segments in chunks]
    return pl.pallas_call(
        functools.partial(order_rest_kernel, chunks, devices),
        name="order_rest",
        in_specs=[SM, VM, VM],
        out_specs=[VM] * (1 + len(chunks)),
        out_shape=[jax.ShapeDtypeStruct(col.shape, BF16)]
        + [jax.ShapeDtypeStruct((rows, w), BF16) for w in widths],
        compiler_params=params(16),
        cost_estimate=cost(2 * rows * rows * rows, 4 * rows * rows),
    )(me, row, col)


def levels_kernel(edges, with_columns, me_ref, ev_ref, mat_ref, *rest):
    fo_refs, rest = rest[: 2 if edges else 1], rest[2 if edges else 1 :]
    col_ref, outs = (rest[0], rest[1:]) if with_columns else (None, rest)
    per, blocks, sub, width = ev_ref.shape
    own = outs[0].shape[1]
    late = (pl.program_id(0) >= pl.num_programs(0) // 2).astype(jnp.int32)
    near = late != (me_ref[0] & 1)
    mat = mat_ref[...]
    for r in range(per):
        following = fo_refs[0][r * blocks : (r + 1) * blocks]
        if edges:
            following = jnp.where(near, fo_refs[1][r * blocks : (r + 1) * blocks], following)
        hi, lo = split((ev_ref[r] - following).reshape(blocks * sub, width))
        mixed = mm(mat, hi) + mm(mat, lo)
        if with_columns:
            hi, lo = split(mixed)
            mixed = mm(hi, col_ref[...]) + mm(lo, col_ref[...])
        for s, ref in enumerate(outs):
            ref[r] = mixed[s * own : (s + 1) * own]


def mix_levels(count, me, evolved, following, mat, col=None):
    rows, blocks, sub, width = evolved.shape
    levels = blocks * sub
    own = levels // count
    per = 2
    edges = len(following) == 2
    half = rows // (2 * per)
    spec = pl.BlockSpec((per * blocks, sub, width), lambda i: (lax.rem(i, half) if edges else i, 0, 0))
    cols = [] if col is None else [col]
    return pl.pallas_call(
        functools.partial(levels_kernel, edges, col is not None),
        name="mix_levels",
        grid=(rows // per,),
        in_specs=[
            SM,
            pl.BlockSpec((per, blocks, sub, width), lambda i: (i, 0, 0, 0)),
            pl.BlockSpec(mat.shape, lambda i: (0, 0)),
        ]
        + [spec] * len(following)
        + [pl.BlockSpec(c.shape, lambda i: (0, 0)) for c in cols],
        out_specs=[pl.BlockSpec((per, own, width), lambda i: (i, 0, 0))] * count,
        out_shape=[jax.ShapeDtypeStruct((rows, own, width), F32)] * count,
        compiler_params=params(16),
        cost_estimate=cost(4 * levels * levels * rows * width, 12 * evolved.size),
    )(me, evolved, mat, *following, *cols)


def by_level(x):
    groups = [turn([x[g + i] for i in range(SUB)]) for g in range(0, x.shape[0], SUB)]
    return [jnp.concatenate([g[z] for g in groups], axis=0) for z in range(SUB)]


def stacked(x):
    return jnp.concatenate(split(x), axis=0)


def rows_kernel(counts, col_ref, *rest):
    mats, xs, out_ref = rest[: len(counts)], rest[len(counts) : -1], rest[-1]
    width = out_ref.shape[2]
    totals = [None] * SUB
    start = 0
    for mat_ref, count in zip(mats, counts):
        x = jnp.concatenate([ref[...] for ref in xs[start : start + count]], axis=0)
        start += count
        depth = x.shape[0]
        hi, lo = split(x.reshape(depth * SUB, width))
        mixed = (mm(hi, col_ref[...]) + mm(lo, col_ref[...])).reshape(depth, SUB, width)
        for z, level in enumerate(by_level(mixed)):
            part = mm(mat_ref[...], stacked(level))
            totals[z] = part if totals[z] is None else totals[z] + part
    for z in range(SUB):
        out_ref[z] = totals[z]


def mix_rows(col, mats, groups):
    blocks = [x for group in groups for x in group]
    own, width = blocks[0].shape[1:]
    rows = mats[0].shape[0]
    depth = sum(x.shape[0] for x in blocks)
    return pl.pallas_call(
        functools.partial(rows_kernel, [len(g) for g in groups]),
        name="mix_rows",
        grid=(own // SUB,),
        in_specs=[pl.BlockSpec(m.shape, lambda i: (0, 0)) for m in [col, *mats]]
        + [pl.BlockSpec((x.shape[0], SUB, width), lambda i: (0, i, 0)) for x in blocks],
        out_specs=pl.BlockSpec((SUB, rows, width), lambda i: (i, 0, 0)),
        out_shape=jax.ShapeDtypeStruct((own, rows, width), F32),
        compiler_params=params(36),
        cost_estimate=cost(4 * own * depth * width * (width + rows), 4 * own * width * (depth + rows)),
    )(col, *mats, *blocks)


def finish_kernel(count, mat_ref, base_ref, *rest):
    out_ref = rest[-1]
    x = jnp.concatenate([ref[...] for ref in rest[:count]], axis=0)
    for z, level in enumerate(by_level(x)):
        out_ref[z] = base_ref[z] + mm(mat_ref[...], stacked(level))


def finish(part, mat, base, blocks, out=None):
    _, rows, width = base.shape
    cols = 2 * LANES if width % (2 * LANES) == 0 else LANES
    spec = pl.BlockSpec((SUB, rows, cols), lambda j: (part, 0, j))
    rest = [] if out is None else [out]
    depth = sum(x.shape[0] for x in blocks)
    return pl.pallas_call(
        functools.partial(finish_kernel, len(blocks)),
        name="finish",
        grid=(width // cols,),
        in_specs=[pl.BlockSpec(mat.shape, lambda j: (0, 0)), spec]
        + [pl.BlockSpec((x.shape[0], SUB, cols), lambda j: (0, 0, j)) for x in blocks]
        + [ANY] * len(rest),
        out_specs=spec,
        out_shape=jax.ShapeDtypeStruct(base.shape, F32),
        input_output_aliases={2 + len(blocks): 0} if rest else {},
        compiler_params=params(16),
        cost_estimate=cost(4 * SUB * depth * rows * width, 4 * SUB * width * (depth + 2 * rows)),
    )(mat, base, *blocks, *rest)


def tiled_body(increment, diffusivity, wind, vertical_cov, row_cov, column_cov):
    raw, kappa = increment[0], diffusivity[0]
    devices, windows = lax.axis_size("tile"), lax.axis_size("win")
    levels, rows, _ = raw.shape
    blocks = levels // SUB
    me = lax.axis_index("tile").astype(jnp.int32)
    half_wind = jnp.broadcast_to((0.5 * wind[0]).reshape(SUB, blocks).T[:, :, None], (blocks, SUB, LANES))
    inside = jnp.stack([me != 0, me != devices - 1]).astype(F32)
    half = rows // 2
    side = half - FIRST // 2 - HALO
    cuts = ((half - FIRST // 2, FIRST), (HALO, side), (half + FIRST // 2, side))
    chunks = tuple((c,) for c in cuts) + (((0, HALO), (rows - HALO, HALO)),)
    one = me.reshape(1)
    far = far_edge(raw, kappa, one)
    *parts, near, kappa = pieces(raw, kappa, cuts, one)

    def earlier(x):
        return lax.ppermute(x, "win", [(i + 1, i) for i in range(windows - 1)])

    apart = [(t, t + 1) for t in range(1, devices - 1, 2)] + [(t + 1, t) for t in range(1, devices - 1, 2)]
    far_in = lax.ppermute(far, "tile", apart)
    follow = [earlier(parts[0])]
    follow.append(earlier(parts[1]))
    near_in = lax.ppermute(near, "tile", [(t, t ^ 1) for t in range(devices)])
    level_mat = order_levels(devices, one, vertical_cov)

    def exchange(mixed):
        got = [mixed[0]] + [None] * (devices - 1)
        for span in (range(devices // 2, devices), range(devices // 2 - 1, 0, -1)):
            for s in span:
                got[s] = lax.ppermute(mixed[s], "tile", [(t, t ^ s) for t in range(devices)])
        return got

    groups = []
    own = [*parts, far, near]
    for j, (first, count) in enumerate(cuts):
        ev = steps([first], count, one, inside, half_wind, kappa, cuts, own)
        mixed = mix_levels(devices, one, ev, [follow[j]], level_mat)
        groups.append(exchange(mixed))
        *own, _ = lax.optimization_barrier((*own, mixed[0]))
        if j == 0:
            follow.append(earlier(own[2]))
        elif j == 1:
            row, col, _ = lax.optimization_barrier((row_cov, column_cov, mixed[0]))
            col_mat, *row_mats = order_rest(chunks, devices, one, row, col)
            follow_edges = [earlier(own[3]), earlier(own[4])]
    ev = steps([0, rows - HALO], HALO, one, inside, half_wind, kappa, cuts, own, [far_in, near_in])
    halves = levels // devices // SUB
    mixed = mix_levels(devices * halves, one, ev, follow_edges, level_mat, col_mat)
    base = mix_rows(col_mat, row_mats[:3], groups)
    out = None
    for h in range(halves):
        last = exchange(mixed[h::halves])
        out = finish(h, row_mats[3], base, last, out)
    return out[None]


def with_halo(cells, sides, width):
    for axis, dim in sides:
        count = lax.axis_size(axis)
        ends = count - 1
        head = lax.slice_in_dim(cells, 0, width, axis=dim)
        tail = lax.slice_in_dim(cells, cells.shape[dim] - width, cells.shape[dim], axis=dim)
        cells = jnp.concatenate(
            [
                lax.ppermute(tail, axis, [(i, (i + 1) % count) for i in range(ends)]),
                cells,
                lax.ppermute(head, axis, [((i + 1) % count, i) for i in range(ends)]),
            ],
            axis=dim,
        )
    return cells


def tendency(center, north, south, kappa, wind_col):
    east = jnp.roll(center, -1, axis=2)
    west = jnp.roll(center, 1, axis=2)
    stacked = jnp.pad(center, ((1, 1), (0, 0), (0, 0)))
    horiz = north + south + east + west - 4.0 * center
    vert = stacked[2:] + stacked[:-2] - 2.0 * center
    return center + kappa[None] * horiz + VMIX * vert + wind_col * (0.5 * (south - north))


def plain_body(increment, diffusivity, wind, vertical_cov, row_cov, column_cov):
    field, kappa, wind_col = increment[0], diffusivity[0], wind[0][:, None, None]
    current = field
    for _ in range(STEPS):
        padded = with_halo(current, (("tile", 1),), 1)
        current = tendency(current, padded[:, 2:], padded[:, :-2], kappa, wind_col)
    size = lax.axis_size("win")
    defect = current - lax.ppermute(field, "win", [(i + 1, i) for i in range(size - 1)])
    levels, rows, width = defect.shape
    high = lax.Precision.HIGHEST
    mixed = jnp.dot(vertical_cov.astype(F32), defect.reshape(levels, rows * width), precision=high)
    mixed = jnp.dot(mixed.reshape(levels * rows, width), column_cov.astype(F32), precision=high)
    mixed = lax.all_to_all(mixed.reshape(levels, rows, width), "tile", split_axis=0, concat_axis=1, tiled=True)
    return jnp.einsum("yk,zkx->zyx", row_cov.astype(F32), mixed, precision=high)[None]


def body(*args):
    levels, rows, width = args[0].shape[1:]
    devices = lax.axis_size("tile")
    own = levels // devices
    fits = (
        rows >= 2 * HALO + 2 * SUB + FIRST
        and rows % SUB == 0
        and levels % (2 * SUB) == 0
        and levels % devices == 0
        and own % SUB == 0
        and width % LANES == 0
        and devices & (devices - 1) == 0
        and devices % SUB == 0
    )
    return tiled_body(*args) if fits else plain_body(*args)


def solution(mesh):
    in_specs = (P("win", None, "tile", None), P("win", "tile", None), P("win", None), P(), P(), P())
    out_specs = P("win", "tile", None, None)


    return jax.shard_map(body, mesh=mesh, in_specs=in_specs, out_specs=out_specs, check_vma=False)
```
